32 devices in a mesh: seq: 8 (over y, x, core), head: 4 (over z).
Axes of the slice: x: 2, y: 2, z: 4, core: 2. Of those that a mesh axis runs over, the one named last changes fastest.
Arguments:
- ssm_input: bfloat16 [1536, 16384], P('seq', 'head'), may hold values from -6 to 6
- state_in: bfloat16 [1536, 2048], P('seq'), may hold values from -0.375 to 0.375
- state_out: bfloat16 [1536, 2048], P('seq'), may hold values from -0.15625 to 0.15625
- step_size: float32 [1536, 256], P('seq', 'head'), may hold values from 0.5 to 1.5
- decay_rate: float32 [256], P('head'), may hold values from 3.25520833e-05 to 0.04
- forget: float32 [1536], P('seq'), may hold values from 0 to 0.9
- skip_gain: float32 [256], P('head'), may hold values from 0.25 to 1.75
- queries: bfloat16 [1536, 8192], P('seq', 'head'), may hold values from -48 to 48
- new_keys: bfloat16 [1536, 1024], P('seq'), may hold values from -6 to 6
- new_values: bfloat16 [1536, 1024], P('seq'), may hold values from -6 to 6
- cache_keys: bfloat16 [1024, 1024], P('seq'), may hold values from -127 to 127, as said below
- cache_values: bfloat16 [1024, 1024], P('seq'), may hold values from -127 to 127, as said below
- cache_key_scale: float32 [1024], replicated, may hold values from 0.003 to 0.03
- cache_value_scale: float32 [1024], replicated, may hold values from 0.003 to 0.03
Outputs:
- ssm_output: bfloat16 [1536, 16384], P('seq', 'head')
- attended: bfloat16 [1536, 8192], P('seq', 'head')
- key_codes: bfloat16 [1536, 1024], P('seq')
- key_scale: float32 [1024], replicated
The draws below stay inside these ranges and needn't reach their ends.
Inputs may be any that keep to these rules, and one draw needn't show every extreme that they name: `cache_keys`: whole numbers. `cache_values`: whole numbers.
All inputs are finite; a program needn't handle non-finite values.
Results may differ from the reference program's by a relative error of at most 0.019.
Values may be sent and summed in bfloat16 or wider, within the bound.
A program may use at most 128 MiB of HBM per device.

```python
import math
import jax
import jax.numpy as jnp
from jax import lax

SSM_HEADS = 256
HEAD_DIM = 64
STATE = 256
GROUPS = 8
ATT_HEADS = 64
KV_HEADS = 8
ATT_DIM = 128
TOK_DEV = 192
TOKENS = 1536
CACHE = 1024


def draw_decay_rate(key, part):
    key_a, key_b, key_c = jax.random.split(jax.random.fold_in(key, 11), 3)
    slow = jnp.exp(jax.random.uniform(key_a, (SSM_HEADS,), minval=math.log(0.05 / TOKENS), maxval=math.log(0.4 / TOKENS)))
    quick = jax.random.uniform(key_b, (SSM_HEADS,), minval=0.02, maxval=0.04)
    share = 0.5
    picked = jax.random.uniform(key_c, (SSM_HEADS,)) < share
    return jnp.where(picked, quick, slow).astype(jnp.float32)


def draw_forget(key, part):
    key_a, key_b = jax.random.split(jax.random.fold_in(key, 12), 2)
    spots = jax.random.randint(key_a, (4,), 0, TOKENS)
    amount = jax.random.uniform(key_b, (4,), minval=0.2, maxval=0.4)
    hits = (jnp.arange(TOKENS, dtype=jnp.int32)[:, None] == spots[None, :]).astype(jnp.float32)
    return jnp.dot(hits, amount).astype(jnp.float32)


def draw_queries(key, part):
    key_a = jax.random.fold_in(jax.random.fold_in(key, 13), 0)
    base = jax.random.normal(key_a, (TOKENS, ATT_HEADS * ATT_DIM))
    return jnp.clip(base, -48.0, 48.0).astype(jnp.bfloat16)


def cache_codes(key):
    spread = jax.random.uniform(key, (CACHE, KV_HEADS * ATT_DIM), minval=-127.0, maxval=127.0)
    return jnp.clip(jnp.floor(spread + 0.5), -127.0, 127.0).astype(jnp.bfloat16)


def draw_cache_keys(key, part):
    return cache_codes(jax.random.fold_in(key, 14))


def draw_cache_values(key, part):
    return cache_codes(jax.random.fold_in(key, 15))


def block_scale(own_key, dims, cuts, smallest, high):
    factor_of, own = 1.0, jax.random.fold_in(own_key, 6)
    for axis_at, parts in cuts:
        draws = jnp.exp(jax.random.uniform(jax.random.fold_in(own, axis_at), (parts,), jnp.float32, smallest / len(cuts), high / len(cuts)))
        factor_of = factor_of * jnp.repeat(draws, dims[axis_at] // parts).reshape([-1 if axis == axis_at else 1 for axis in range(len(dims))])
    return factor_of


def bell_draw(key, shape, scale, limit, pieces=(), kind=jnp.bfloat16):
    array = scale * jax.random.normal(key, shape, jnp.float32)
    if pieces:
        array = array * block_scale(key, shape, pieces, -0.22, 0.18)
    return jnp.clip(array, -limit, limit).astype(kind)


def setup_inputs(seed: int = 0) -> dict:
    key_list = jax.random.split(jax.random.key(seed), 15)
    return {
        "ssm_input": bell_draw(key_list[0], (TOKENS, SSM_HEADS * HEAD_DIM), 1.0, 6.0, ((0, 8), (1, 4))),
        "state_in": bell_draw(key_list[1], (TOKENS, GROUPS * STATE), STATE ** -0.5, 0.375, ((0, 8),)),
        "state_out": bell_draw(key_list[2], (TOKENS, GROUPS * STATE), TOKENS ** -0.5, 0.15625, ((0, 8),)),
        "step_size": jnp.clip(0.5 + 1.0 * jax.random.uniform(key_list[3], (TOKENS, SSM_HEADS), jnp.float32) ** block_scale(key_list[3], (TOKENS, SSM_HEADS), ((0, 8), (1, 4)), -0.2, 0.2), 0.5, 1.5),
        "decay_rate": draw_decay_rate(jax.random.fold_in(key_list[14], 71), 0),
        "forget": draw_forget(jax.random.fold_in(key_list[14], 71), 0),
        "skip_gain": jnp.clip(1.0 + 0.15 * jax.random.normal(key_list[6], (SSM_HEADS,), jnp.float32), 0.25, 1.75),
        "queries": draw_queries(jax.random.fold_in(key_list[14], 71), 0),
        "new_keys": bell_draw(key_list[8], (TOKENS, KV_HEADS * ATT_DIM), 1.0, 6.0, ((0, 8),)),
        "new_values": bell_draw(key_list[9], (TOKENS, KV_HEADS * ATT_DIM), 1.0, 6.0, ((0, 8),)),
        "cache_keys": draw_cache_keys(jax.random.fold_in(key_list[14], 71), 0),
        "cache_values": draw_cache_values(jax.random.fold_in(key_list[14], 71), 0),
        "cache_key_scale": jnp.clip(jnp.exp(jax.random.uniform(key_list[12], (KV_HEADS * ATT_DIM,), jnp.float32, math.log(0.003), math.log(0.03))), 0.003, 0.03),
        "cache_value_scale": jnp.clip(jnp.exp(jax.random.uniform(key_list[13], (KV_HEADS * ATT_DIM,), jnp.float32, math.log(0.003), math.log(0.03))), 0.003, 0.03),
    }


NEG = -1.0e30


def head_maps(maps, choose):
    highest = lax.Precision.HIGHEST
    length = maps.shape[0]
    grouped = maps.reshape(length, GROUPS, STATE)
    return jnp.einsum('tgn,hg->thn', grouped, choose, precision=highest)


def span_parts(rate, inputs, in_heads, out_heads):
    highest = lax.Precision.HIGHEST
    length = rate.shape[0]
    lower = jnp.tril(jnp.ones((length, length), jnp.float32))
    running = jnp.dot(lower, rate, precision=highest)
    gram = jnp.einsum('thn,shn->hts', out_heads, in_heads, precision=highest)
    across = running.T
    spread = across[:, :, None] - across[:, None, :]
    causal = lower[None, :, :] > 0.0
    weight = jnp.where(causal, jnp.exp(jnp.where(causal, spread, 0.0)), 0.0) * gram
    within = jnp.einsum('hts,shp->thp', weight, inputs, precision=highest)
    final = running[length - 1]
    tail = jnp.exp(final[None, :] - running)
    local = jnp.einsum('sh,shp,shn->hpn', tail, inputs, in_heads, precision=highest)
    return running, within, local, jnp.exp(final)


def prior_term(running, out_heads, carried):
    highest = lax.Precision.HIGHEST
    return jnp.exp(running)[:, :, None] * jnp.einsum('thn,hpn->thp', out_heads, carried, precision=highest)


def ssd_layer(ssm_input, state_in, state_out, step_size, decay_rate, forget, skip_gain):
    blocks = TOKENS // TOK_DEV
    rate = -decay_rate[None, :] * step_size - forget[:, None]
    signal = ssm_input.astype(jnp.float32).reshape(TOKENS, SSM_HEADS, HEAD_DIM)
    inputs = signal * step_size[:, :, None]
    head_group = jnp.arange(SSM_HEADS, dtype=jnp.int32) // (SSM_HEADS // GROUPS)
    choose = (head_group[:, None] == jnp.arange(GROUPS, dtype=jnp.int32)[None, :]).astype(jnp.float32)

    def advance(carried, item):
        rate_b, input_b, in_b, out_b, signal_b = item
        in_heads = head_maps(in_b, choose)
        out_heads = head_maps(out_b, choose)
        running, within, local, decay = span_parts(rate_b, input_b, in_heads, out_heads)
        mixed = within + prior_term(running, out_heads, carried) + skip_gain[None, :, None] * signal_b
        carried = decay[:, None, None] * carried + local
        return carried, mixed

    start = jnp.zeros((SSM_HEADS, HEAD_DIM, STATE), jnp.float32)
    items = (rate.reshape(blocks, TOK_DEV, SSM_HEADS),
             inputs.reshape(blocks, TOK_DEV, SSM_HEADS, HEAD_DIM),
             state_in.astype(jnp.float32).reshape(blocks, TOK_DEV, GROUPS * STATE),
             state_out.astype(jnp.float32).reshape(blocks, TOK_DEV, GROUPS * STATE),
             signal.reshape(blocks, TOK_DEV, SSM_HEADS, HEAD_DIM))
    _, mixed = lax.scan(advance, start, items)
    return mixed.reshape(TOKENS, SSM_HEADS * HEAD_DIM).astype(jnp.bfloat16)


def attention_layer(queries, new_keys, new_values, cache_keys, cache_values, cache_key_scale, cache_value_scale):
    cache_k = (cache_keys.astype(jnp.float32) * cache_key_scale[None, :]).astype(jnp.bfloat16)
    cache_v = (cache_values.astype(jnp.float32) * cache_value_scale[None, :]).astype(jnp.bfloat16)
    keys = jnp.concatenate([cache_k, new_keys], axis=0).reshape(CACHE + TOKENS, KV_HEADS, ATT_DIM)
    values = jnp.concatenate([cache_v, new_values], axis=0).reshape(CACHE + TOKENS, KV_HEADS, ATT_DIM)
    heads = queries.reshape(TOKENS, ATT_HEADS, ATT_DIM)
    group = ATT_HEADS // KV_HEADS
    key_pos = jnp.arange(CACHE + TOKENS, dtype=jnp.int32)
    query_pos = CACHE + jnp.arange(TOKENS, dtype=jnp.int32)
    visible = key_pos[None, :] <= query_pos[:, None]

    def one_head(index):
        query = lax.dynamic_index_in_dim(heads, index, axis=1, keepdims=False)
        key_head = lax.dynamic_index_in_dim(keys, index // group, axis=1, keepdims=False)
        value_head = lax.dynamic_index_in_dim(values, index // group, axis=1, keepdims=False)
        scores = jnp.dot(query, key_head.T, preferred_element_type=jnp.float32) * (ATT_DIM ** -0.5)
        scores = jnp.where(visible, scores, NEG)
        peak = jnp.max(scores, axis=1, keepdims=True)
        weights = jnp.where(visible, jnp.exp(scores - peak), 0.0)
        total = jnp.sum(weights, axis=1, keepdims=True)
        summed = jnp.dot(weights.astype(jnp.bfloat16), value_head, preferred_element_type=jnp.float32)
        return (summed / total).astype(jnp.bfloat16)

    outputs = lax.map(one_head, jnp.arange(ATT_HEADS, dtype=jnp.int32))
    return outputs.transpose(1, 0, 2).reshape(TOKENS, ATT_HEADS * ATT_DIM)


def reference(ssm_input, state_in, state_out, step_size, decay_rate, forget, skip_gain, queries, new_keys, new_values, cache_keys, cache_values, cache_key_scale, cache_value_scale):
    ssm_output = ssd_layer(ssm_input, state_in, state_out, step_size, decay_rate, forget, skip_gain)
    attended = attention_layer(queries, new_keys, new_values, cache_keys, cache_values, cache_key_scale, cache_value_scale)
    magnitude = jnp.max(jnp.abs(new_keys.astype(jnp.float32)), axis=0)
    key_scale = (magnitude + 1e-6) / 127.0
    key_codes = (new_keys.astype(jnp.float32) / key_scale[None, :]).astype(jnp.bfloat16)
    return ssm_output, attended, key_codes, key_scale
```

```python
import functools
import jax
import jax.numpy as jnp
from jax import lax
from jax.experimental import pallas as pl
from jax.experimental.pallas import tpu as pltpu
from jax.sharding import PartitionSpec as P

SSM_HEADS = 256
HEAD_DIM = 64
STATE = 256
GROUPS = 8
ATT_HEADS = 64
KV_HEADS = 8
ATT_DIM = 128

NEG = -1e30
LOG2E = 1.4426950408889634
HIGHEST = lax.Precision.HIGHEST
MESH = pl.DeviceIdType.MESH
VMEM = pl.BlockSpec(memory_space=pltpu.VMEM)
F32 = jnp.float32
BF16 = jnp.bfloat16


def iota(shape, axis):
    return lax.broadcasted_iota(jnp.int32, shape, axis)


def lanes(start, size):
    return pl.ds(pl.multiple_of(start, 128), size)


def local_kernel(
    x_ref,
    sin_ref,
    sout_ref,
    step_ref,
    decay_ref,
    forget_ref,
    skip_ref,
    nk_ref,
    nv_ref,
    ck_ref,
    cv_ref,
    cks_ref,
    cvs_ref,
    state_ref,
    part_ref,
    fade_ref,
    meta_ref,
    kvc_ref,
    kvn_ref,
    gram_ref,
    bt_ref,
    at_ref,
):
    tokens, width = x_ref.shape
    heads = step_ref.shape[1]
    per_group = min(SSM_HEADS // GROUPS, heads)
    groups_here = heads // per_group
    z = lax.axis_index("head")
    group0 = z * heads // (SSM_HEADS // GROUPS)
    kvw = kvc_ref.shape[1] // 2
    q_heads = heads * ATT_HEADS // SSM_HEADS
    first = z * q_heads // (ATT_HEADS // KV_HEADS)
    cols = lanes(first * ATT_DIM, kvw)
    kvc_ref[:, :kvw] = (ck_ref[:, cols].astype(F32) * cks_ref[:, cols]).astype(BF16)
    kvc_ref[:, kvw:] = (cv_ref[:, cols].astype(F32) * cvs_ref[:, cols]).astype(BF16)
    kvn_ref[:, :kvw] = nk_ref[:, cols]
    kvn_ref[:, kvw:] = nv_ref[:, cols]
    meta_ref[:, width:] = jnp.max(jnp.abs(nk_ref[...].astype(F32)), axis=0, keepdims=True)

    rate = (-decay_ref[...] * step_ref[...] - forget_ref[...]) * LOG2E
    row, col = iota((tokens, tokens), 0), iota((tokens, tokens), 1)
    lower = jnp.where(col <= row, 1.0, 0.0)
    eye = jnp.where(col == row, 1.0, 0.0)
    running = jnp.dot(lower, rate, precision=HIGHEST, preferred_element_type=F32)
    lstep = jnp.log2(step_ref[...])
    start = running - lstep
    at_ref[...] = lax.dot_general(
        start, eye, (((0,), (0,)), ((), ())), precision=HIGHEST, preferred_element_type=F32
    )
    tail = jnp.exp2(running[tokens - 1 : tokens] - start).astype(BF16)
    for g in range(groups_here):
        gcols = lanes((group0 + g) * STATE, STATE)
        maps_in = sin_ref[:, gcols]
        gram_ref[g] = lax.dot_general(
            sout_ref[:, gcols], maps_in, (((1,), (1,)), ((), ())), preferred_element_type=F32
        )
        bt_ref[g] = lax.dot_general(
            maps_in,
            eye.astype(BF16),
            (((0,), (0,)), ((), ())),
            preferred_element_type=F32,
        ).astype(BF16)

    def pair(p, _):
        here = lanes(p * 128, 128)
        g = (2 * p) // per_group
        pick = (iota((heads, 128), 0) == 2 * p + iota((heads, 128), 1) // HEAD_DIM).astype(F32)
        run = jnp.dot(running, pick, precision=HIGHEST, preferred_element_type=F32)
        meta_ref[:, here] = run[tokens - 1 : tokens]
        fade_ref[:, here] = jnp.exp2(run).astype(BF16)
        x = x_ref[:, here]
        scale = jnp.dot(tail, pick.astype(BF16), preferred_element_type=F32)
        scaled = (x.astype(F32) * scale).astype(BF16)
        state_ref[:, here] = jnp.dot(
            bt_ref[g], scaled, preferred_element_type=F32
        ).astype(BF16)
        gram = gram_ref[g]
        causal = iota((tokens, tokens), 1) <= iota((tokens, tokens), 0)

        def one(k):
            spread = run[:, k * HEAD_DIM : k * HEAD_DIM + 1] - at_ref[pl.ds(2 * p + k, 1), :]
            weight = jnp.exp2(jnp.where(causal, spread, NEG)) * gram
            return jnp.dot(weight.astype(BF16), x, preferred_element_type=F32)

        y = jnp.where(iota((tokens, 128), 1) < HEAD_DIM, one(0), one(1))
        part_ref[:, here] = (y + skip_ref[:, here] * x.astype(F32)).astype(BF16)
        return 0

    lax.fori_loop(0, heads // 2, pair, 0)


def comm_kernel(
    n,
    chunks,
    state_ref,
    kvc_ref,
    kvn_ref,
    meta_ref,
    out_ref,
    allc_ref,
    alln_ref,
    allm_ref,
    sib_ref,
    own_ref,
    incl_ref,
    recv_ref,
    back_ref,
    meta_s,
    meta_r,
    kv_s,
    kv_r,
    kv_f,
    sib_s,
    sib_r,
    pre_s,
    pre_r,
    rel_s,
    back_s,
    back_r,
):
    n2 = n // 2
    levels = n2.bit_length() - 1
    me = lax.axis_index("seq")
    i, c = me % 2, me // 2
    other = me + 1 - 2 * i
    width = state_ref.shape[1]
    half = width // 2
    size = half // chunks

    barrier = pltpu.get_barrier_semaphore()
    for d in range(1, n):
        pl.semaphore_signal(
            barrier, inc=1, device_id={"seq": (me + d) % n}, device_id_type=MESH
        )
    pl.semaphore_wait(barrier, n - 1)

    def remote(src, dst, ssem, rsem, to):
        return pltpu.make_async_remote_copy(
            src_ref=src,
            dst_ref=dst,
            send_sem=ssem,
            recv_sem=rsem,
            device_id={"seq": to},
            device_id_type=MESH,
        )

    def sib_copy(j):
        return remote(
            state_ref.at[:, lanes((1 - i) * half + j * size, size)],
            sib_ref.at[j],
            sib_s.at[j],
            sib_r.at[j],
            other,
        )

    for j in range(chunks):
        sib_copy(j).start()
    for d in range(1, n):
        remote(
            meta_ref, allm_ref.at[me], meta_s.at[d], meta_r.at[me], (me + d) % n
        ).start()

    def cache_copy(d, to):
        return remote(kvc_ref, allc_ref.at[me], kv_s.at[0, d], kv_r.at[0, me], to)

    def new_copy(d, to):
        return remote(kvn_ref, alln_ref.at[me], kv_s.at[1, d], kv_r.at[1, me], to)

    cache_copy(0, other).start()
    new_copy(0, other).start()
    for d in range(1, n2):
        to = ((c + d) % n2) * 2 + i
        cache_copy(d, to).start()

        @pl.when(c + d < n2)
        def _():
            new_copy(d, to).start()

    allm_ref[me] = meta_ref[...]
    allc_ref[me] = kvc_ref[...]
    alln_ref[me] = kvn_ref[...]
    for d in range(1, n2):
        later = c + d

        @pl.when(later < n2)
        def _():
            for k in range(2):
                alln_ref[later * 2 + k] = jnp.zeros(kvn_ref.shape, BF16)

    for d in range(1, n):
        r = (me + d) % n
        remote(meta_ref, allm_ref.at[r], meta_s.at[d], meta_r.at[r], r).wait_recv()

    def sends(l):
        return c % (2 ** (l + 1)) == 2**l - 1

    def targets(l):
        return [0] if l == 0 else list(range(1, 2**l, 2))

    def pre_copy(l, j, r):
        return remote(
            incl_ref.at[l, j],
            recv_ref.at[l, j],
            pre_s.at[l, j, r],
            pre_r.at[l, j],
            ((c + 1 + r) % n2) * 2 + i,
        )

    def relay_copy(l, j):
        return remote(
            recv_ref.at[l, j],
            recv_ref.at[l, j],
            rel_s.at[l, j],
            pre_r.at[l, j],
            ((c + n2 - 1) % n2) * 2 + i,
        )

    def logs(r, j):
        return allm_ref[r, :, lanes(i * half + j * size, size)]

    def gather_first(j, _):
        sib_copy(j).wait_recv()
        mine = state_ref[:, lanes(i * half + j * size, size)].astype(F32)
        theirs = sib_ref[j].astype(F32)
        d1 = jnp.exp2(logs(2 * c + 1, j))
        total = jnp.where(i == 0, d1 * mine + theirs, d1 * theirs + mine)
        incl_ref[0, j] = total.astype(BF16)
        own_ref[j] = jnp.zeros(own_ref.shape[1:], F32)

        @pl.when(sends(0))
        def _():
            pre_copy(0, j, 0).start()

        return 0

    lax.fori_loop(0, chunks, gather_first, 0)

    def forward(kind, d):
        src = allc_ref if kind == 0 else alln_ref
        slot = ((c + d) % n2) * 2 + i
        return remote(
            src.at[slot], src.at[slot], kv_f.at[kind, d], kv_r.at[kind, slot], other
        )

    def combine(j, _):
        for l in range(levels):

            @pl.when(c % (2 ** (l + 1)) >= 2**l)
            def _():
                pre_copy(l, j, 0).wait_recv()
                if l >= 1:

                    @pl.when(c % 2 == 1)
                    def _():
                        relay_copy(l, j).start()

                base = c - c % (2**l)
                logsum = jnp.zeros((1, size), F32)
                for back in range(1, 2**l):
                    at = (c + n2 - back) % n2
                    both = logs(2 * at, j) + logs(2 * at + 1, j)
                    logsum += jnp.where(c - back >= base, both, 0.0)
                own_ref[j] = jnp.exp2(logsum) * recv_ref[l, j].astype(F32) + own_ref[j]

            if l + 1 < levels:

                @pl.when(sends(l + 1))
                def _():
                    keep = jnp.exp2(logs(2 * c, j) + logs(2 * c + 1, j))
                    incl_ref[l + 1, j] = (
                        keep * own_ref[j] + incl_ref[0, j].astype(F32)
                    ).astype(BF16)
                    for r in targets(l + 1):
                        pre_copy(l + 1, j, r).start()

        enter = own_ref[j]
        mine = state_ref[:, lanes(i * half + j * size, size)].astype(F32)
        first = jnp.where(i == 0, mine, sib_ref[j].astype(F32))
        middle = jnp.exp2(logs(2 * c, j)) * enter + first
        out_ref[:, lanes(i * half + j * size, size)] = jnp.where(
            i == 0, enter, middle
        ).astype(BF16)
        back_ref[j] = jnp.where(i == 0, middle, enter).astype(BF16)
        back_copy(j, i).start()
        for d in range(1, n2):

            @pl.when(j == ((d * chunks) // n2))
            def _():
                remote_slot(0, d).wait_recv()
                forward(0, d).start()

                @pl.when((c + d) % n2 < c)
                def _():
                    remote_slot(1, d).wait_recv()
                    forward(1, d).start()

        return 0

    def remote_slot(kind, d):
        src = allc_ref if kind == 0 else alln_ref
        mine = kvc_ref if kind == 0 else kvn_ref
        slot = ((c + d) % n2) * 2 + i
        return remote(mine, src.at[slot], kv_s.at[kind, d], kv_r.at[kind, slot], slot)

    def back_copy(j, who):
        return remote(
            back_ref.at[j],
            out_ref.at[:, lanes(who * half + j * size, size)],
            back_s.at[j],
            back_r.at[j],
            other,
        )

    lax.fori_loop(0, chunks, combine, 0)

    def other_slot(kind, d):
        src = allc_ref if kind == 0 else alln_ref
        mine = kvc_ref if kind == 0 else kvn_ref
        slot = ((c + d) % n2) * 2 + (1 - i)
        return remote(mine, src.at[slot], kv_f.at[kind, d], kv_r.at[kind, slot], other)

    for d in range(n2):
        other_slot(0, d).wait_recv()
    other_slot(1, 0).wait_recv()
    for d in range(1, n2):

        @pl.when((c + d) % n2 < c)
        def _():
            other_slot(1, d).wait_recv()

    def drain(j, _):
        back_copy(j, 1 - i).wait_recv()
        back_copy(j, i).wait_send()
        sib_copy(j).wait_send()
        for l in range(levels):

            @pl.when(sends(l))
            def _():
                for r in targets(l):
                    pre_copy(l, j, r).wait_send()

            if l >= 1:

                @pl.when((c % (2 ** (l + 1)) >= 2**l) & (c % 2 == 1))
                def _():
                    relay_copy(l, j).wait_send()

        return 0

    lax.fori_loop(0, chunks, drain, 0)
    for d in range(1, n):
        remote(
            meta_ref, allm_ref.at[me], meta_s.at[d], meta_r.at[me], (me + d) % n
        ).wait_send()
    cache_copy(0, other).wait_send()
    new_copy(0, other).wait_send()
    for d in range(1, n2):
        to = ((c + d) % n2) * 2 + i
        cache_copy(d, to).wait_send()
        forward(0, d).wait_send()

        @pl.when(c + d < n2)
        def _():
            new_copy(d, to).wait_send()

        @pl.when((c + d) % n2 < c)
        def _():
            forward(1, d).wait_send()


def final_kernel(
    part_ref,
    fade_ref,
    sout_ref,
    state_ref,
    q_ref,
    kvc_ref,
    kvn_ref,
    meta_ref,
    nk_ref,
    y_ref,
    att_ref,
    code_ref,
    scale_ref,
    vc_ref,
    vn_ref,
    bias_ref,
):
    tokens, width = part_ref.shape
    heads = width // HEAD_DIM
    per_group = min(SSM_HEADS // GROUPS, heads)
    me, z = lax.axis_index("seq"), lax.axis_index("head")
    group0 = z * heads // (SSM_HEADS // GROUPS)
    block = min(512, width)

    magnitude = jnp.max(meta_ref[:, 0, width:], axis=0, keepdims=True)
    scale = (magnitude + 1e-6) / 127.0
    scale_ref[...] = scale
    code_ref[...] = (nk_ref[...].astype(F32) / scale).astype(BF16)

    def columns(b, _):
        here = lanes(b * block, block)
        g = group0 + (b * block) // (per_group * HEAD_DIM)
        prior = jnp.dot(
            sout_ref[:, lanes(g * STATE, STATE)], state_ref[:, here], preferred_element_type=F32
        )
        y = part_ref[:, here].astype(F32) + fade_ref[:, here].astype(F32) * prior
        y_ref[:, here] = y.astype(BF16)
        return 0

    lax.fori_loop(0, width // block, columns, 0)

    q_heads = q_ref.shape[1] // ATT_DIM
    kvw = kvc_ref.shape[1] // 2
    kv_here = kvw // ATT_DIM
    share = q_heads // kv_here
    fresh = kvn_ref.shape[0]
    for k in range(kv_here):
        at = kvw + k * ATT_DIM
        vc_ref[k, :, :ATT_DIM] = kvc_ref[:, at : at + ATT_DIM]
        vc_ref[k, :, ATT_DIM:] = jnp.ones((kvc_ref.shape[0], ATT_DIM), BF16)
        vn_ref[k, :, :ATT_DIM] = kvn_ref[:, at : at + ATT_DIM]
        vn_ref[k, :, ATT_DIM:] = jnp.ones((fresh, ATT_DIM), BF16)
    seen = iota((tokens, fresh), 1) <= me * tokens + iota((tokens, fresh), 0)
    bias_ref[...] = jnp.where(seen, 0.0, NEG)
    factor = ATT_DIM**-0.5 * LOG2E
    nt = (((1,), (1,)), ((), ()))

    def attend(h, _):
        k = h // share
        q = q_ref[:, lanes(h * ATT_DIM, ATT_DIM)]
        at = lanes(k * ATT_DIM, ATT_DIM)
        old = lax.dot_general(q, kvc_ref[:, at], nt, preferred_element_type=F32)
        new = lax.dot_general(q, kvn_ref[:, at], nt, preferred_element_type=F32) + bias_ref[...]
        peak = jnp.maximum(
            jnp.max(old, axis=1, keepdims=True), jnp.max(new, axis=1, keepdims=True)
        )
        old = jnp.exp2((old - peak) * factor).astype(BF16)
        new = jnp.exp2((new - peak) * factor).astype(BF16)
        both = jnp.dot(old, vc_ref[k], preferred_element_type=F32) + jnp.dot(
            new, vn_ref[k], preferred_element_type=F32
        )
        att_ref[:, lanes(h * ATT_DIM, ATT_DIM)] = (
            both[:, :ATT_DIM] / both[:, ATT_DIM:]
        ).astype(BF16)
        return 0

    lax.fori_loop(0, q_heads, attend, 0)


def body(
    n,
    ssm_input,
    state_in,
    state_out,
    step_size,
    decay_rate,
    forget,
    skip_gain,
    queries,
    new_keys,
    new_values,
    cache_keys,
    cache_values,
    cache_key_scale,
    cache_value_scale,
):
    tokens, width = ssm_input.shape
    heads = step_size.shape[1]
    rows = cache_keys.shape[0]
    channels = new_keys.shape[1]
    q_heads = queries.shape[1] // ATT_DIM
    kv_here = max(1, q_heads // (ATT_HEADS // KV_HEADS))
    kvw = kv_here * ATT_DIM
    per_group = min(SSM_HEADS // GROUPS, heads)
    groups_here = heads // per_group
    limit = pltpu.CompilerParams(vmem_limit_bytes=60 * 1024 * 1024)
    shape = jax.ShapeDtypeStruct
    state, part, fade, meta, kvc, kvn = pl.pallas_call(
        local_kernel,
        out_shape=(
            shape((STATE, width), BF16),
            shape((tokens, width), BF16),
            shape((tokens, width), BF16),
            shape((1, width + channels), F32),
            shape((rows, 2 * kvw), BF16),
            shape((tokens, 2 * kvw), BF16),
        ),
        in_specs=[VMEM] * 13,
        out_specs=(VMEM,) * 6,
        scratch_shapes=[
            pltpu.VMEM((groups_here, tokens, tokens), F32),
            pltpu.VMEM((groups_here, STATE, tokens), BF16),
            pltpu.VMEM((heads, tokens), F32),
        ],
        compiler_params=limit,
        name="local",
    )(
        ssm_input,
        state_in,
        state_out,
        step_size,
        decay_rate.reshape(1, heads),
        forget.reshape(tokens, 1),
        jnp.repeat(skip_gain, HEAD_DIM).reshape(1, width),
        new_keys,
        new_values,
        cache_keys,
        cache_values,
        cache_key_scale.reshape(1, channels),
        cache_value_scale.reshape(1, channels),
    )
    half = width // 2
    size = min(256, half)
    chunks = half // size
    n2 = n // 2
    levels = n2.bit_length() - 1
    fan = max(1, n2 // 2)
    dma = pltpu.SemaphoreType.DMA
    carried, allc, alln, allm = pl.pallas_call(
        functools.partial(comm_kernel, n, chunks),
        out_shape=(
            shape((STATE, width), BF16),
            shape((n, rows, 2 * kvw), BF16),
            shape((n, tokens, 2 * kvw), BF16),
            shape((n, 1, width + channels), F32),
        ),
        in_specs=[VMEM] * 4,
        out_specs=(VMEM,) * 4,
        scratch_shapes=[
            pltpu.VMEM((chunks, STATE, size), BF16),
            pltpu.VMEM((chunks, STATE, size), F32),
            pltpu.VMEM((levels, chunks, STATE, size), BF16),
            pltpu.VMEM((levels, chunks, STATE, size), BF16),
            pltpu.VMEM((chunks, STATE, size), BF16),
            dma((n,)),
            dma((n,)),
            dma((2, n2)),
            dma((2, n)),
            dma((2, n2)),
            dma((chunks,)),
            dma((chunks,)),
            dma((levels, chunks, fan)),
            dma((levels, chunks)),
            dma((levels, chunks)),
            dma((chunks,)),
            dma((chunks,)),
        ],
        compiler_params=pltpu.CompilerParams(
            collective_id=0, has_side_effects=True, vmem_limit_bytes=60 * 1024 * 1024
        ),
        name="exchange",
    )(state, kvc, kvn, meta)
    y, attended, codes, scale = pl.pallas_call(
        final_kernel,
        out_shape=(
            shape((tokens, width), BF16),
            shape((tokens, queries.shape[1]), BF16),
            shape((tokens, channels), BF16),
            shape((1, channels), F32),
        ),
        in_specs=[VMEM] * 9,
        out_specs=(VMEM,) * 4,
        scratch_shapes=[
            pltpu.VMEM((kv_here, n * rows, 2 * ATT_DIM), BF16),
            pltpu.VMEM((kv_here, n * tokens, 2 * ATT_DIM), BF16),
            pltpu.VMEM((tokens, n * tokens), F32),
        ],
        compiler_params=limit,
        name="finish",
    )(
        part,
        fade,
        state_out,
        carried,
        queries,
        allc.reshape(n * rows, 2 * kvw),
        alln.reshape(n * tokens, 2 * kvw),
        allm,
        new_keys,
    )
    return (y, attended, codes, scale.reshape(channels))


def solution(mesh):
    in_specs = (
        P("seq", "head"),
        P("seq", None),
        P("seq", None),
        P("seq", "head"),
        P("head"),
        P("seq"),
        P("head"),
        P("seq", "head"),
        P("seq", None),
        P("seq", None),
        P("seq", None),
        P("seq", None),
        P(),
        P(),
    )
    out_specs = (P("seq", "head"), P("seq", "head"), P("seq", None), P())
    return jax.shard_map(
        functools.partial(body, mesh.shape["seq"]),
        mesh=mesh,
        in_specs=in_specs,
        out_specs=out_specs,
        check_vma=False,
    )
```

```python
import functools
import jax
import jax.numpy as jnp
from jax import lax
from jax.experimental import pallas as pl
from jax.experimental.pallas import tpu as pltpu
from jax.sharding import PartitionSpec as P

SSM_HEADS = 256
HEAD_DIM = 64
STATE = 256
GROUPS = 8
ATT_HEADS = 64
KV_HEADS = 8
ATT_DIM = 128

NEG = -1e30
LOG2E = 1.4426950408889634
HIGHEST = lax.Precision.HIGHEST
MESH = pl.DeviceIdType.MESH
VMEM = pl.BlockSpec(memory_space=pltpu.VMEM)
F32 = jnp.float32
BF16 = jnp.bfloat16


def iota(shape, axis):
    return lax.broadcasted_iota(jnp.int32, shape, axis)


def lanes(start, size):
    return pl.ds(pl.multiple_of(start, 128), size)


def local_kernel(
    x_ref,
    sin_ref,
    sout_ref,
    step_ref,
    decay_ref,
    forget_ref,
    skip_ref,
    nk_ref,
    nv_ref,
    ck_ref,
    cv_ref,
    cks_ref,
    cvs_ref,
    state_ref,
    run_ref,
    at_ref,
    gram_ref,
    meta_ref,
    kvc_ref,
    kvn_ref,
):
    tokens, width = x_ref.shape
    heads = step_ref.shape[0]
    per_group = min(SSM_HEADS // GROUPS, heads)
    groups_here = heads // per_group
    z = lax.axis_index("head")
    group0 = z * heads // (SSM_HEADS // GROUPS)
    kvw = kvc_ref.shape[1] // 2
    q_heads = heads * ATT_HEADS // SSM_HEADS
    first = z * q_heads // (ATT_HEADS // KV_HEADS)
    cols = lanes(first * ATT_DIM, kvw)
    kvc_ref[:, :kvw] = (ck_ref[:, cols].astype(F32) * cks_ref[:, cols]).astype(BF16)
    kvc_ref[:, kvw:] = (cv_ref[:, cols].astype(F32) * cvs_ref[:, cols]).astype(BF16)
    kvn_ref[:, :kvw] = nk_ref[:, cols]
    kvn_ref[:, kvw:] = nv_ref[:, cols]
    meta_ref[:, width:] = jnp.max(jnp.abs(nk_ref[...].astype(F32)), axis=0, keepdims=True)

    row, col = iota((tokens, tokens), 0), iota((tokens, tokens), 1)
    lower = jnp.where(col <= row, 1.0, 0.0)
    eye = jnp.where(col == row, 1.0, 0.0)
    step = step_ref[...].T
    forgotten = jnp.sum(lower * forget_ref[...], axis=1, keepdims=True)
    decayed = jnp.dot(
        lower, decay_ref[...] * step, precision=HIGHEST, preferred_element_type=F32
    )
    running = -(decayed + forgotten) * LOG2E
    start = running - jnp.log2(step)
    at_ref[...] = start.T
    run_ref[:tokens] = running
    run_ref[tokens:] = jnp.broadcast_to(skip_ref[...], (8, heads))
    tail = jnp.exp2(running[tokens - 1 : tokens] - start).astype(BF16)
    last = running[tokens - 8 : tokens]
    block = min(512, width)
    for g in range(groups_here):
        gcols = lanes((group0 + g) * STATE, STATE)
        maps_in = sin_ref[:, gcols]
        gram_ref[g] = lax.dot_general(
            sout_ref[:, gcols], maps_in, (((1,), (1,)), ((), ())), preferred_element_type=F32
        )
        turned = lax.dot_general(
            maps_in,
            eye.astype(BF16),
            (((0,), (0,)), ((), ())),
            preferred_element_type=F32,
        ).astype(BF16)
        for b in range(per_group * HEAD_DIM // block):
            begin = g * per_group * HEAD_DIM + b * block
            here = pl.ds(begin, block)
            pick = choose(heads, begin, block)
            meta_ref[:, here] = jnp.dot(
                last, pick, precision=HIGHEST, preferred_element_type=F32
            )[7:8]
            scale = jnp.dot(tail, pick.astype(BF16), preferred_element_type=F32)
            scaled = (x_ref[:, here].astype(F32) * scale).astype(BF16)
            state_ref[:, here] = jnp.dot(
                turned, scaled, preferred_element_type=F32
            ).astype(BF16)


def choose(heads, begin, size):
    lane = begin + iota((heads, size), 1)
    return (iota((heads, size), 0) == lane // HEAD_DIM).astype(F32)


def within_pair(p, x_ref, run_ref, at_ref, gram_ref, part_ref):
    tokens = x_ref.shape[0]
    heads = run_ref.shape[1]
    per_group = min(SSM_HEADS // GROUPS, heads)
    here = lanes(p * 128, 128)
    pick = choose(heads, p * 128, 128)
    both = jnp.dot(run_ref[...], pick, precision=HIGHEST, preferred_element_type=F32)
    run, skip = both[:tokens], both[tokens : tokens + 1]
    x = x_ref[:, here]
    gram = gram_ref[(2 * p) // per_group]
    causal = iota((tokens, tokens), 1) <= iota((tokens, tokens), 0)

    def one(k):
        spread = run[:, k * HEAD_DIM : k * HEAD_DIM + 1] - at_ref[pl.ds(2 * p + k, 1), :]
        weight = jnp.exp2(jnp.where(causal, spread, NEG)) * gram
        return jnp.dot(weight.astype(BF16), x, preferred_element_type=F32)

    y = jnp.where(iota((tokens, 128), 1) < HEAD_DIM, one(0), one(1))
    part_ref[:, here] = (y + skip * x.astype(F32)).astype(BF16)


def attend(h, q_ref, allc_ref, alln_ref, bias_ref, vc_ref, vn_ref, att_ref):
    q_heads = q_ref.shape[1] // ATT_DIM
    kv_here = vc_ref.shape[0]
    k = h // (q_heads // kv_here)
    factor = ATT_DIM**-0.5 * LOG2E
    nt = (((1,), (1,)), ((), ()))
    q = q_ref[:, lanes(h * ATT_DIM, ATT_DIM)]
    at = lanes(k * ATT_DIM, ATT_DIM)
    keys_c = allc_ref[:, :, at].reshape(-1, ATT_DIM)
    keys_n = alln_ref[:, :, at].reshape(-1, ATT_DIM)
    old = lax.dot_general(q, keys_c, nt, preferred_element_type=F32)
    new = lax.dot_general(q, keys_n, nt, preferred_element_type=F32) + bias_ref[...]
    peak = jnp.maximum(
        jnp.max(old, axis=1, keepdims=True), jnp.max(new, axis=1, keepdims=True)
    )
    old = jnp.exp2((old - peak) * factor).astype(BF16)
    new = jnp.exp2((new - peak) * factor).astype(BF16)
    both = jnp.dot(old, vc_ref[k], preferred_element_type=F32) + jnp.dot(
        new, vn_ref[k], preferred_element_type=F32
    )
    att_ref[:, lanes(h * ATT_DIM, ATT_DIM)] = (
        both[:, :ATT_DIM] / both[:, ATT_DIM:]
    ).astype(BF16)


def comm_kernel(
    n,
    chunks,
    state_ref,
    kvc_ref,
    kvn_ref,
    meta_ref,
    x_ref,
    run_ref,
    at_ref,
    gram_ref,
    q_ref,
    out_ref,
    allm_ref,
    part_ref,
    att_ref,
    allc_ref,
    alln_ref,
    vc_ref,
    vn_ref,
    bias_ref,
    sib_ref,
    own_ref,
    incl_ref,
    recv_ref,
    back_ref,
    meta_s,
    meta_r,
    kv_s,
    kv_r,
    kv_f,
    sib_s,
    sib_r,
    pre_s,
    pre_r,
    rel_s,
    back_s,
    back_r,
):
    n2 = n // 2
    levels = n2.bit_length() - 1
    me = lax.axis_index("seq")
    i, c = me % 2, me // 2
    other = me + 1 - 2 * i
    width = state_ref.shape[1]
    half = width // 2
    size = half // chunks

    barrier = pltpu.get_barrier_semaphore()
    for d in range(1, n):
        pl.semaphore_signal(
            barrier, inc=1, device_id={"seq": (me + d) % n}, device_id_type=MESH
        )
    pl.semaphore_wait(barrier, n - 1)

    def remote(src, dst, ssem, rsem, to):
        return pltpu.make_async_remote_copy(
            src_ref=src,
            dst_ref=dst,
            send_sem=ssem,
            recv_sem=rsem,
            device_id={"seq": to},
            device_id_type=MESH,
        )

    def sib_copy(j):
        return remote(
            state_ref.at[:, lanes((1 - i) * half + j * size, size)],
            sib_ref.at[j],
            sib_s.at[j],
            sib_r.at[j],
            other,
        )

    for j in range(chunks):
        sib_copy(j).start()
    for d in range(1, n):
        remote(
            meta_ref, allm_ref.at[me], meta_s.at[d], meta_r.at[me], (me + d) % n
        ).start()

    def cache_copy(d, to):
        return remote(kvc_ref, allc_ref.at[me], kv_s.at[0, d], kv_r.at[0, me], to)

    def new_copy(d, to):
        return remote(kvn_ref, alln_ref.at[me], kv_s.at[1, d], kv_r.at[1, me], to)

    cache_copy(0, other).start()
    new_copy(0, other).start()
    for d in range(1, n2):
        to = ((c + d) % n2) * 2 + i
        cache_copy(d, to).start()

        @pl.when(c + d < n2)
        def _():
            new_copy(d, to).start()

    allm_ref[me] = meta_ref[...]
    allc_ref[me] = kvc_ref[...]
    alln_ref[me] = kvn_ref[...]
    for d in range(1, n2):
        later = c + d

        @pl.when(later < n2)
        def _():
            for k in range(2):
                alln_ref[later * 2 + k] = jnp.zeros(kvn_ref.shape, BF16)

    for d in range(1, n):
        r = (me + d) % n
        remote(meta_ref, allm_ref.at[r], meta_s.at[d], meta_r.at[r], r).wait_recv()

    def sends(l):
        return c % (2 ** (l + 1)) == 2**l - 1

    def targets(l):
        return [0] if l == 0 else list(range(1, 2**l, 2))

    def pre_copy(l, j, r):
        return remote(
            incl_ref.at[l, j],
            recv_ref.at[l, j],
            pre_s.at[l, j, r],
            pre_r.at[l, j],
            ((c + 1 + r) % n2) * 2 + i,
        )

    def relay_copy(l, j):
        return remote(
            recv_ref.at[l, j],
            recv_ref.at[l, j],
            rel_s.at[l, j],
            pre_r.at[l, j],
            ((c + n2 - 1) % n2) * 2 + i,
        )

    def logs(r, j):
        return allm_ref[r, :, lanes(i * half + j * size, size)]

    def gather_first(j, _):
        sib_copy(j).wait_recv()
        mine = state_ref[:, lanes(i * half + j * size, size)].astype(F32)
        theirs = sib_ref[j].astype(F32)
        d1 = jnp.exp2(logs(2 * c + 1, j))
        total = jnp.where(i == 0, d1 * mine + theirs, d1 * theirs + mine)
        incl_ref[0, j] = total.astype(BF16)
        own_ref[j] = jnp.zeros(own_ref.shape[1:], F32)

        @pl.when(sends(0))
        def _():
            pre_copy(0, j, 0).start()

        return 0

    lax.fori_loop(0, chunks, gather_first, 0)
    fresh = bias_ref.shape[1]
    tokens = x_ref.shape[0]
    seen = iota((tokens, fresh), 1) <= me * tokens + iota((tokens, fresh), 0)
    bias_ref[...] = jnp.where(seen, 0.0, NEG)
    early = max(1, chunks // 2)
    late = max(1, chunks - early)

    def forward(kind, d):
        src = allc_ref if kind == 0 else alln_ref
        slot = ((c + d) % n2) * 2 + i
        return remote(
            src.at[slot], src.at[slot], kv_f.at[kind, d], kv_r.at[kind, slot], other
        )

    def combine(j, _):
        for l in range(levels):

            @pl.when(c % (2 ** (l + 1)) >= 2**l)
            def _():
                pre_copy(l, j, 0).wait_recv()
                if l >= 1:

                    @pl.when(c % 2 == 1)
                    def _():
                        relay_copy(l, j).start()

                base = c - c % (2**l)
                logsum = jnp.zeros((1, size), F32)
                for back in range(1, 2**l):
                    at = (c + n2 - back) % n2
                    both = logs(2 * at, j) + logs(2 * at + 1, j)
                    logsum += jnp.where(c - back >= base, both, 0.0)
                own_ref[j] = jnp.exp2(logsum) * recv_ref[l, j].astype(F32) + own_ref[j]

            if l + 1 < levels:

                @pl.when(sends(l + 1))
                def _():
                    keep = jnp.exp2(logs(2 * c, j) + logs(2 * c + 1, j))
                    incl_ref[l + 1, j] = (
                        keep * own_ref[j] + incl_ref[0, j].astype(F32)
                    ).astype(BF16)
                    for r in targets(l + 1):
                        pre_copy(l + 1, j, r).start()

        enter = own_ref[j]
        mine = state_ref[:, lanes(i * half + j * size, size)].astype(F32)
        first = jnp.where(i == 0, mine, sib_ref[j].astype(F32))
        middle = jnp.exp2(logs(2 * c, j)) * enter + first
        out_ref[:, lanes(i * half + j * size, size)] = jnp.where(
            i == 0, enter, middle
        ).astype(BF16)
        back_ref[j] = jnp.where(i == 0, middle, enter).astype(BF16)
        back_copy(j, i).start()
        return 0

    def remote_slot(kind, d):
        src = allc_ref if kind == 0 else alln_ref
        mine = kvc_ref if kind == 0 else kvn_ref
        slot = ((c + d) % n2) * 2 + i
        return remote(mine, src.at[slot], kv_s.at[kind, d], kv_r.at[kind, slot], slot)

    def back_copy(j, who):
        return remote(
            back_ref.at[j],
            out_ref.at[:, lanes(who * half + j * size, size)],
            back_s.at[j],
            back_r.at[j],
            other,
        )

    def first_part(j, _):
        pairs = width // 128

        def pair(p, _):
            within_pair(p, x_ref, run_ref, at_ref, gram_ref, part_ref)
            return 0

        lax.fori_loop(j * pairs // early, (j + 1) * pairs // early, pair, 0)
        combine(j, 0)
        for d in range(1, n2):

            @pl.when(j == (d * early) // n2)
            def _():
                remote_slot(0, d).wait_recv()
                forward(0, d).start()

                @pl.when((c + d) % n2 < c)
                def _():
                    remote_slot(1, d).wait_recv()
                    forward(1, d).start()

        return 0

    lax.fori_loop(0, early, first_part, 0)

    def other_slot(kind, d):
        src = allc_ref if kind == 0 else alln_ref
        mine = kvc_ref if kind == 0 else kvn_ref
        slot = ((c + d) % n2) * 2 + (1 - i)
        return remote(mine, src.at[slot], kv_f.at[kind, d], kv_r.at[kind, slot], other)

    for d in range(n2):
        other_slot(0, d).wait_recv()
    other_slot(1, 0).wait_recv()
    for d in range(1, n2):

        @pl.when((c + d) % n2 < c)
        def _():
            other_slot(1, d).wait_recv()

    kv_here = vc_ref.shape[0]
    for k in range(kv_here):
        at = (kv_here + k) * ATT_DIM
        for all_ref, ext_ref in ((allc_ref, vc_ref), (alln_ref, vn_ref)):
            ext_ref[k, :, :ATT_DIM] = all_ref[:, :, at : at + ATT_DIM].reshape(-1, ATT_DIM)
            ext_ref[k, :, ATT_DIM:] = jnp.ones((ext_ref.shape[1], ATT_DIM), BF16)

    def second_part(j, _):
        q_heads = q_ref.shape[1] // ATT_DIM

        def head(h, _):
            attend(h, q_ref, allc_ref, alln_ref, bias_ref, vc_ref, vn_ref, att_ref)
            return 0

        lax.fori_loop(j * q_heads // late, (j + 1) * q_heads // late, head, 0)

        @pl.when(early + j < chunks)
        def _():
            combine(early + j, 0)

        return 0

    lax.fori_loop(0, late, second_part, 0)

    def drain(j, _):
        back_copy(j, 1 - i).wait_recv()
        back_copy(j, i).wait_send()
        sib_copy(j).wait_send()
        for l in range(levels):

            @pl.when(sends(l))
            def _():
                for r in targets(l):
                    pre_copy(l, j, r).wait_send()

            if l >= 1:

                @pl.when((c % (2 ** (l + 1)) >= 2**l) & (c % 2 == 1))
                def _():
                    relay_copy(l, j).wait_send()

        return 0

    lax.fori_loop(0, chunks, drain, 0)
    for d in range(1, n):
        remote(
            meta_ref, allm_ref.at[me], meta_s.at[d], meta_r.at[me], (me + d) % n
        ).wait_send()
    cache_copy(0, other).wait_send()
    new_copy(0, other).wait_send()
    for d in range(1, n2):
        to = ((c + d) % n2) * 2 + i
        cache_copy(d, to).wait_send()
        forward(0, d).wait_send()

        @pl.when(c + d < n2)
        def _():
            new_copy(d, to).wait_send()

        @pl.when((c + d) % n2 < c)
        def _():
            forward(1, d).wait_send()


def final_kernel(
    part_ref,
    run_ref,
    sout_ref,
    state_ref,
    meta_ref,
    nk_ref,
    y_ref,
    code_ref,
    scale_ref,
):
    tokens, width = part_ref.shape
    heads = run_ref.shape[1]
    per_group = min(SSM_HEADS // GROUPS, heads)
    z = lax.axis_index("head")
    group0 = z * heads // (SSM_HEADS // GROUPS)
    block = min(512, width)

    magnitude = jnp.max(meta_ref[:, 0, width:], axis=0, keepdims=True)
    scale = (magnitude + 1e-6) / 127.0
    scale_ref[...] = scale
    code_ref[...] = (nk_ref[...].astype(F32) / scale).astype(BF16)
    fade = jnp.exp2(run_ref[:tokens]).astype(BF16)
    for b in range(width // block):
        here = pl.ds(b * block, block)
        g = group0 + (b * block) // (per_group * HEAD_DIM)
        prior = jnp.dot(
            sout_ref[:, lanes(g * STATE, STATE)], state_ref[:, here], preferred_element_type=F32
        )
        pick = choose(heads, b * block, block).astype(BF16)
        spread = jnp.dot(fade, pick, preferred_element_type=F32)
        y_ref[:, here] = (part_ref[:, here].astype(F32) + spread * prior).astype(BF16)


def body(
    n,
    ssm_input,
    state_in,
    state_out,
    step_size,
    decay_rate,
    forget,
    skip_gain,
    queries,
    new_keys,
    new_values,
    cache_keys,
    cache_values,
    cache_key_scale,
    cache_value_scale,
):
    tokens, width = ssm_input.shape
    heads = step_size.shape[1]
    rows = cache_keys.shape[0]
    channels = new_keys.shape[1]
    q_heads = queries.shape[1] // ATT_DIM
    kv_here = max(1, q_heads // (ATT_HEADS // KV_HEADS))
    kvw = kv_here * ATT_DIM
    per_group = min(SSM_HEADS // GROUPS, heads)
    groups_here = heads // per_group
    limit = pltpu.CompilerParams(vmem_limit_bytes=60 * 1024 * 1024)
    shape = jax.ShapeDtypeStruct
    state, run, at, gram, meta, kvc, kvn = pl.pallas_call(
        local_kernel,
        out_shape=(
            shape((STATE, width), BF16),
            shape((tokens + 8, heads), F32),
            shape((heads, tokens), F32),
            shape((groups_here, tokens, tokens), F32),
            shape((1, width + channels), F32),
            shape((rows, 2 * kvw), BF16),
            shape((tokens, 2 * kvw), BF16),
        ),
        in_specs=[VMEM] * 13,
        out_specs=(VMEM,) * 7,
        compiler_params=limit,
        name="local",
    )(
        ssm_input,
        state_in,
        state_out,
        step_size.T,
        decay_rate.reshape(1, heads),
        forget.reshape(1, tokens),
        skip_gain.reshape(1, heads),
        new_keys,
        new_values,
        cache_keys,
        cache_values,
        cache_key_scale.reshape(1, channels),
        cache_value_scale.reshape(1, channels),
    )
    half = width // 2
    size = min(256, half)
    chunks = half // size
    n2 = n // 2
    levels = n2.bit_length() - 1
    fan = max(1, n2 // 2)
    dma = pltpu.SemaphoreType.DMA
    carried, allm, part, attended = pl.pallas_call(
        functools.partial(comm_kernel, n, chunks),
        out_shape=(
            shape((STATE, width), BF16),
            shape((n, 1, width + channels), F32),
            shape((tokens, width), BF16),
            shape((tokens, queries.shape[1]), BF16),
        ),
        in_specs=[VMEM] * 9,
        out_specs=(VMEM,) * 4,
        scratch_shapes=[
            pltpu.VMEM((n, rows, 2 * kvw), BF16),
            pltpu.VMEM((n, tokens, 2 * kvw), BF16),
            pltpu.VMEM((kv_here, n * rows, 2 * ATT_DIM), BF16),
            pltpu.VMEM((kv_here, n * tokens, 2 * ATT_DIM), BF16),
            pltpu.VMEM((tokens, n * tokens), F32),
            pltpu.VMEM((chunks, STATE, size), BF16),
            pltpu.VMEM((chunks, STATE, size), F32),
            pltpu.VMEM((levels, chunks, STATE, size), BF16),
            pltpu.VMEM((levels, chunks, STATE, size), BF16),
            pltpu.VMEM((chunks, STATE, size), BF16),
            dma((n,)),
            dma((n,)),
            dma((2, n2)),
            dma((2, n)),
            dma((2, n2)),
            dma((chunks,)),
            dma((chunks,)),
            dma((levels, chunks, fan)),
            dma((levels, chunks)),
            dma((levels, chunks)),
            dma((chunks,)),
            dma((chunks,)),
        ],
        compiler_params=pltpu.CompilerParams(
            collective_id=0, has_side_effects=True, vmem_limit_bytes=60 * 1024 * 1024
        ),
        name="exchange",
    )(state, kvc, kvn, meta, ssm_input, run, at, gram, queries)
    y, codes, scale = pl.pallas_call(
        final_kernel,
        out_shape=(
            shape((tokens, width), BF16),
            shape((tokens, channels), BF16),
            shape((1, channels), F32),
        ),
        in_specs=[VMEM] * 6,
        out_specs=(VMEM,) * 3,
        compiler_params=limit,
        name="finish",
    )(part, run, state_out, carried, allm, new_keys)
    return (y, attended, codes, scale.reshape(channels))


def solution(mesh):
    in_specs = (
        P("seq", "head"),
        P("seq", None),
        P("seq", None),
        P("seq", "head"),
        P("head"),
        P("seq"),
        P("head"),
        P("seq", "head"),
        P("seq", None),
        P("seq", None),
        P("seq", None),
        P("seq", None),
        P(),
        P(),
    )
    out_specs = (P("seq", "head"), P("seq", "head"), P("seq", None), P())
    return jax.shard_map(
        functools.partial(body, mesh.shape["seq"]),
        mesh=mesh,
        in_specs=in_specs,
        out_specs=out_specs,
        check_vma=False,
    )
```

```python
import functools
import jax
import jax.numpy as jnp
from jax import lax
from jax.experimental import pallas as pl
from jax.experimental.pallas import tpu as pltpu
from jax.sharding import PartitionSpec as P

SSM_HEADS = 256
HEAD_DIM = 64
STATE = 256
GROUPS = 8
ATT_HEADS = 64
KV_HEADS = 8
ATT_DIM = 128

NEG = -1e30
LOG2E = 1.4426950408889634
HIGHEST = lax.Precision.HIGHEST
MESH = pl.DeviceIdType.MESH
VMEM = pl.BlockSpec(memory_space=pltpu.VMEM)
F32 = jnp.float32
BF16 = jnp.bfloat16


def iota(shape, axis):
    return lax.broadcasted_iota(jnp.int32, shape, axis)


def lanes(start, size):
    return pl.ds(pl.multiple_of(start, 128), size)


def local_kernel(
    x_ref,
    sin_ref,
    sout_ref,
    step_ref,
    decay_ref,
    forget_ref,
    skip_ref,
    nk_ref,
    nv_ref,
    ck_ref,
    cv_ref,
    cks_ref,
    cvs_ref,
    state_ref,
    run_ref,
    fade_ref,
    at_ref,
    gram_ref,
    meta_ref,
    kvc_ref,
    kvn_ref,
):
    tokens, width = x_ref.shape
    heads = step_ref.shape[0]
    per_group = min(SSM_HEADS // GROUPS, heads)
    groups_here = heads // per_group
    z = lax.axis_index("head")
    group0 = z * heads // (SSM_HEADS // GROUPS)
    kvw = kvc_ref.shape[1] // 2
    q_heads = heads * ATT_HEADS // SSM_HEADS
    first = z * q_heads // (ATT_HEADS // KV_HEADS)
    cols = lanes(first * ATT_DIM, kvw)
    kvc_ref[:, :kvw] = (ck_ref[:, cols].astype(F32) * cks_ref[:, cols]).astype(BF16)
    kvc_ref[:, kvw:] = (cv_ref[:, cols].astype(F32) * cvs_ref[:, cols]).astype(BF16)
    kvn_ref[:, :kvw] = nk_ref[:, cols]
    kvn_ref[:, kvw:] = nv_ref[:, cols]
    meta_ref[:, width:] = jnp.max(jnp.abs(nk_ref[...].astype(F32)), axis=0, keepdims=True)

    row, col = iota((tokens, tokens), 0), iota((tokens, tokens), 1)
    lower = jnp.where(col <= row, 1.0, 0.0)
    eye = jnp.where(col == row, 1.0, 0.0)
    step = step_ref[...].T
    forgotten = jnp.sum(lower * forget_ref[...], axis=1, keepdims=True)
    decayed = jnp.dot(
        lower, decay_ref[...] * step, precision=HIGHEST, preferred_element_type=F32
    )
    running = -(decayed + forgotten) * LOG2E
    start = running - jnp.log2(step)
    at_ref[...] = start.T
    rest = jnp.concatenate(
        [running, jnp.broadcast_to(skip_ref[...], (16, heads))], axis=0
    )
    for third in range(3):
        piece = rest.astype(BF16)
        run_ref[:, third * heads : (third + 1) * heads] = piece
        rest = rest - piece.astype(F32)
    fade_ref[...] = jnp.exp2(running).astype(BF16)
    tail = jnp.exp2(running[tokens - 1 : tokens] - start).astype(BF16)
    last = running[tokens - 8 : tokens]
    block = min(512, width)
    for g in range(groups_here):
        gcols = lanes((group0 + g) * STATE, STATE)
        maps_in = sin_ref[:, gcols]
        gram_ref[g] = lax.dot_general(
            sout_ref[:, gcols], maps_in, (((1,), (1,)), ((), ())), preferred_element_type=F32
        )
        turned = lax.dot_general(
            maps_in,
            eye.astype(BF16),
            (((0,), (0,)), ((), ())),
            preferred_element_type=F32,
        ).astype(BF16)
        for b in range(per_group * HEAD_DIM // block):
            begin = g * per_group * HEAD_DIM + b * block
            here = pl.ds(begin, block)
            pick = choose(heads, begin, block)
            meta_ref[:, here] = jnp.dot(
                last, pick, precision=HIGHEST, preferred_element_type=F32
            )[7:8]
            scale = jnp.dot(tail, pick.astype(BF16), preferred_element_type=F32)
            scaled = (x_ref[:, here].astype(F32) * scale).astype(BF16)
            state_ref[:, here] = jnp.dot(
                turned, scaled, preferred_element_type=F32
            ).astype(BF16)


def choose(heads, begin, size):
    lane = begin + iota((heads, size), 1)
    return (iota((heads, size), 0) == lane // HEAD_DIM).astype(F32)


def within_pair(p, x_ref, run_ref, at_ref, gram_ref, part_ref):
    tokens = x_ref.shape[0]
    heads = run_ref.shape[1] // 3
    per_group = min(SSM_HEADS // GROUPS, heads)
    here = lanes(p * 128, 128)
    pick = choose(heads, p * 128, 128).astype(BF16)
    both = jnp.dot(
        run_ref[...], jnp.concatenate([pick] * 3, axis=0), preferred_element_type=F32
    )
    run, skip = both[:tokens], both[tokens : tokens + 1]
    x = x_ref[:, here]
    gram = gram_ref[(2 * p) // per_group]
    causal = iota((tokens, tokens), 1) <= iota((tokens, tokens), 0)

    def one(k):
        spread = run[:, k * HEAD_DIM : k * HEAD_DIM + 1] - at_ref[pl.ds(2 * p + k, 1), :]
        return (jnp.exp2(jnp.where(causal, spread, NEG)) * gram).astype(BF16)

    pair = jnp.dot(
        jnp.concatenate([one(0), one(1)], axis=0), x, preferred_element_type=F32
    )
    y = jnp.where(iota((tokens, 128), 1) < HEAD_DIM, pair[:tokens], pair[tokens:])
    part_ref[:, here] = (y + skip * x.astype(F32)).astype(BF16)


def attend(h, q_ref, allc_ref, alln_ref, bias_ref, vc_ref, vn_ref, att_ref):
    q_heads = q_ref.shape[1] // ATT_DIM
    kv_here = vc_ref.shape[0]
    share = q_heads // kv_here
    together = 2 if share % 2 == 0 else 1
    tokens = q_ref.shape[0]
    k = (h * together) // share
    factor = ATT_DIM**-0.5 * LOG2E
    nt = (((1,), (1,)), ((), ()))
    own = [lanes((h * together + e) * ATT_DIM, ATT_DIM) for e in range(together)]
    q = jnp.concatenate([q_ref[:, o] for o in own], axis=0)
    at = lanes(k * ATT_DIM, ATT_DIM)
    keys_c = allc_ref[:, :, at].reshape(-1, ATT_DIM)
    keys_n = alln_ref[:, :, at].reshape(-1, ATT_DIM)
    old = lax.dot_general(q, keys_c, nt, preferred_element_type=F32)
    new = lax.dot_general(q, keys_n, nt, preferred_element_type=F32)
    bias = bias_ref[...]
    new = (new.reshape(together, tokens, -1) + bias[None]).reshape(together * tokens, -1)
    peak = jnp.maximum(
        jnp.max(old, axis=1, keepdims=True), jnp.max(new, axis=1, keepdims=True)
    )
    old = jnp.exp2((old - peak) * factor).astype(BF16)
    new = jnp.exp2((new - peak) * factor).astype(BF16)
    both = jnp.dot(old, vc_ref[k], preferred_element_type=F32) + jnp.dot(
        new, vn_ref[k], preferred_element_type=F32
    )
    result = (both[:, :ATT_DIM] / both[:, ATT_DIM:]).astype(BF16)
    for e in range(together):
        att_ref[:, own[e]] = result[e * tokens : (e + 1) * tokens]


def comm_kernel(
    n,
    chunks,
    state_ref,
    kvc_ref,
    kvn_ref,
    meta_ref,
    x_ref,
    run_ref,
    at_ref,
    gram_ref,
    q_ref,
    out_ref,
    allm_ref,
    part_ref,
    att_ref,
    allc_ref,
    alln_ref,
    vc_ref,
    vn_ref,
    bias_ref,
    sib_ref,
    own_ref,
    incl_ref,
    recv_ref,
    back_ref,
    meta_s,
    meta_r,
    kv_s,
    kv_r,
    kv_f,
    sib_s,
    sib_r,
    pre_s,
    pre_r,
    rel_s,
    back_s,
    back_r,
):
    n2 = n // 2
    levels = n2.bit_length() - 1
    me = lax.axis_index("seq")
    i, c = me % 2, me // 2
    other = me + 1 - 2 * i
    width = state_ref.shape[1]
    half = width // 2
    size = half // chunks

    barrier = pltpu.get_barrier_semaphore()
    for d in range(1, n):
        pl.semaphore_signal(
            barrier, inc=1, device_id={"seq": (me + d) % n}, device_id_type=MESH
        )
    pl.semaphore_wait(barrier, n - 1)

    def remote(src, dst, ssem, rsem, to):
        return pltpu.make_async_remote_copy(
            src_ref=src,
            dst_ref=dst,
            send_sem=ssem,
            recv_sem=rsem,
            device_id={"seq": to},
            device_id_type=MESH,
        )

    def sib_copy(j):
        return remote(
            state_ref.at[:, lanes((1 - i) * half + j * size, size)],
            sib_ref.at[j],
            sib_s.at[j],
            sib_r.at[j],
            other,
        )

    for j in range(chunks):
        sib_copy(j).start()
    for d in range(1, n):
        remote(
            meta_ref, allm_ref.at[me], meta_s.at[d], meta_r.at[me], (me + d) % n
        ).start()

    def cache_copy(d, to):
        return remote(kvc_ref, allc_ref.at[me], kv_s.at[0, d], kv_r.at[0, me], to)

    def new_copy(d, to):
        return remote(kvn_ref, alln_ref.at[me], kv_s.at[1, d], kv_r.at[1, me], to)

    cache_copy(0, other).start()
    new_copy(0, other).start()
    for d in range(1, n2):
        to = ((c + d) % n2) * 2 + i
        cache_copy(d, to).start()

        @pl.when(c + d < n2)
        def _():
            new_copy(d, to).start()

    allm_ref[me] = meta_ref[...]
    allc_ref[me] = kvc_ref[...]
    alln_ref[me] = kvn_ref[...]
    for d in range(1, n2):
        later = c + d

        @pl.when(later < n2)
        def _():
            for k in range(2):
                alln_ref[later * 2 + k] = jnp.zeros(kvn_ref.shape, BF16)

    for d in range(1, n):
        r = (me + d) % n
        remote(meta_ref, allm_ref.at[r], meta_s.at[d], meta_r.at[r], r).wait_recv()

    def sends(l):
        return c % (2 ** (l + 1)) == 2**l - 1

    def targets(l):
        return [0] if l == 0 else list(range(1, 2**l, 2))

    def pre_copy(l, j, r):
        return remote(
            incl_ref.at[l, j],
            recv_ref.at[l, j],
            pre_s.at[l, j, r],
            pre_r.at[l, j],
            ((c + 1 + r) % n2) * 2 + i,
        )

    def relay_copy(l, j):
        return remote(
            recv_ref.at[l, j],
            recv_ref.at[l, j],
            rel_s.at[l, j],
            pre_r.at[l, j],
            ((c + n2 - 1) % n2) * 2 + i,
        )

    def logs(r, j):
        return allm_ref[r, :, lanes(i * half + j * size, size)]

    def gather_first(j, _):
        sib_copy(j).wait_recv()
        mine = state_ref[:, lanes(i * half + j * size, size)].astype(F32)
        theirs = sib_ref[j].astype(F32)
        d1 = jnp.exp2(logs(2 * c + 1, j))
        total = jnp.where(i == 0, d1 * mine + theirs, d1 * theirs + mine)
        incl_ref[0, j] = total.astype(BF16)
        own_ref[j] = jnp.zeros(own_ref.shape[1:], F32)

        @pl.when(sends(0))
        def _():
            pre_copy(0, j, 0).start()

        return 0

    lax.fori_loop(0, chunks, gather_first, 0)
    fresh = bias_ref.shape[1]
    tokens = x_ref.shape[0]
    seen = iota((tokens, fresh), 1) <= me * tokens + iota((tokens, fresh), 0)
    bias_ref[...] = jnp.where(seen, 0.0, NEG)
    pairs = width // 128
    early = n2
    ahead = pairs * 3 // 4

    def pair(p, _):
        within_pair(p, x_ref, run_ref, at_ref, gram_ref, part_ref)
        return 0


    def forward(kind, d):
        src = allc_ref if kind == 0 else alln_ref
        slot = ((c + d) % n2) * 2 + i
        return remote(
            src.at[slot], src.at[slot], kv_f.at[kind, d], kv_r.at[kind, slot], other
        )

    def combine(j, _):
        for l in range(levels):

            @pl.when(c % (2 ** (l + 1)) >= 2**l)
            def _():
                pre_copy(l, j, 0).wait_recv()
                if l >= 1:

                    @pl.when(c % 2 == 1)
                    def _():
                        relay_copy(l, j).start()

                base = c - c % (2**l)
                logsum = jnp.zeros((1, size), F32)
                for back in range(1, 2**l):
                    at = (c + n2 - back) % n2
                    both = logs(2 * at, j) + logs(2 * at + 1, j)
                    logsum += jnp.where(c - back >= base, both, 0.0)
                own_ref[j] = jnp.exp2(logsum) * recv_ref[l, j].astype(F32) + own_ref[j]

            if l + 1 < levels:

                @pl.when(sends(l + 1))
                def _():
                    keep = jnp.exp2(logs(2 * c, j) + logs(2 * c + 1, j))
                    incl_ref[l + 1, j] = (
                        keep * own_ref[j] + incl_ref[0, j].astype(F32)
                    ).astype(BF16)
                    for r in targets(l + 1):
                        pre_copy(l + 1, j, r).start()

        enter = own_ref[j]
        mine = state_ref[:, lanes(i * half + j * size, size)].astype(F32)
        first = jnp.where(i == 0, mine, sib_ref[j].astype(F32))
        middle = jnp.exp2(logs(2 * c, j)) * enter + first
        out_ref[:, lanes(i * half + j * size, size)] = jnp.where(
            i == 0, enter, middle
        ).astype(BF16)
        back_ref[j] = jnp.where(i == 0, middle, enter).astype(BF16)
        back_copy(j, i).start()
        return 0

    def remote_slot(kind, d):
        src = allc_ref if kind == 0 else alln_ref
        mine = kvc_ref if kind == 0 else kvn_ref
        slot = ((c + d) % n2) * 2 + i
        return remote(mine, src.at[slot], kv_s.at[kind, d], kv_r.at[kind, slot], slot)

    def back_copy(j, who):
        return remote(
            back_ref.at[j],
            out_ref.at[:, lanes(who * half + j * size, size)],
            back_s.at[j],
            back_r.at[j],
            other,
        )

    def first_part(j, _):
        lax.fori_loop(j * ahead // early, (j + 1) * ahead // early, pair, 0)
        for d in range(1, n2):

            @pl.when(j == d)
            def _():
                remote_slot(0, d).wait_recv()
                forward(0, d).start()

                @pl.when((c + d) % n2 < c)
                def _():
                    remote_slot(1, d).wait_recv()
                    forward(1, d).start()

        return 0

    lax.fori_loop(0, early, first_part, 0)

    def other_slot(kind, d):
        src = allc_ref if kind == 0 else alln_ref
        mine = kvc_ref if kind == 0 else kvn_ref
        slot = ((c + d) % n2) * 2 + (1 - i)
        return remote(mine, src.at[slot], kv_f.at[kind, d], kv_r.at[kind, slot], other)

    for d in range(n2):
        other_slot(0, d).wait_recv()
    other_slot(1, 0).wait_recv()
    for d in range(1, n2):

        @pl.when((c + d) % n2 < c)
        def _():
            other_slot(1, d).wait_recv()

    kv_here = vc_ref.shape[0]
    for k in range(kv_here):
        at = (kv_here + k) * ATT_DIM
        for all_ref, ext_ref in ((allc_ref, vc_ref), (alln_ref, vn_ref)):
            ext_ref[k, :, :ATT_DIM] = all_ref[:, :, at : at + ATT_DIM].reshape(-1, ATT_DIM)
            ext_ref[k, :, ATT_DIM:] = jnp.ones((ext_ref.shape[1], ATT_DIM), BF16)

    q_heads = q_ref.shape[1] // ATT_DIM
    steps = q_heads // 2 if (q_heads // kv_here) % 2 == 0 else q_heads

    def head(h, _):
        attend(h, q_ref, allc_ref, alln_ref, bias_ref, vc_ref, vn_ref, att_ref)
        return 0

    def second_part(j, _):
        rest = pairs - ahead
        lax.fori_loop(
            ahead + j * rest // chunks, ahead + (j + 1) * rest // chunks, pair, 0
        )
        lax.fori_loop(j * steps // chunks, (j + 1) * steps // chunks, head, 0)
        combine(j, 0)
        return 0

    lax.fori_loop(0, chunks, second_part, 0)

    def drain(j, _):
        back_copy(j, 1 - i).wait_recv()
        back_copy(j, i).wait_send()
        sib_copy(j).wait_send()
        for l in range(levels):

            @pl.when(sends(l))
            def _():
                for r in targets(l):
                    pre_copy(l, j, r).wait_send()

            if l >= 1:

                @pl.when((c % (2 ** (l + 1)) >= 2**l) & (c % 2 == 1))
                def _():
                    relay_copy(l, j).wait_send()

        return 0

    lax.fori_loop(0, chunks, drain, 0)
    for d in range(1, n):
        remote(
            meta_ref, allm_ref.at[me], meta_s.at[d], meta_r.at[me], (me + d) % n
        ).wait_send()
    cache_copy(0, other).wait_send()
    new_copy(0, other).wait_send()
    for d in range(1, n2):
        to = ((c + d) % n2) * 2 + i
        cache_copy(d, to).wait_send()
        forward(0, d).wait_send()

        @pl.when(c + d < n2)
        def _():
            new_copy(d, to).wait_send()

        @pl.when((c + d) % n2 < c)
        def _():
            forward(1, d).wait_send()


def final_kernel(
    part_ref,
    fade_ref,
    sout_ref,
    state_ref,
    meta_ref,
    nk_ref,
    y_ref,
    code_ref,
    scale_ref,
):
    tokens, width = part_ref.shape
    heads = fade_ref.shape[1]
    per_group = min(SSM_HEADS // GROUPS, heads)
    z = lax.axis_index("head")
    group0 = z * heads // (SSM_HEADS // GROUPS)
    block = min(512, width)

    magnitude = jnp.max(meta_ref[:, 0, width:], axis=0, keepdims=True)
    scale = (magnitude + 1e-6) / 127.0
    scale_ref[...] = scale
    code_ref[...] = (nk_ref[...].astype(F32) / scale).astype(BF16)
    fade = fade_ref[...]
    for b in range(width // block):
        here = pl.ds(b * block, block)
        g = group0 + (b * block) // (per_group * HEAD_DIM)
        prior = jnp.dot(
            sout_ref[:, lanes(g * STATE, STATE)], state_ref[:, here], preferred_element_type=F32
        )
        pick = choose(heads, b * block, block).astype(BF16)
        spread = jnp.dot(fade, pick, preferred_element_type=F32)
        y_ref[:, here] = (part_ref[:, here].astype(F32) + spread * prior).astype(BF16)


def body(
    n,
    ssm_input,
    state_in,
    state_out,
    step_size,
    decay_rate,
    forget,
    skip_gain,
    queries,
    new_keys,
    new_values,
    cache_keys,
    cache_values,
    cache_key_scale,
    cache_value_scale,
):
    tokens, width = ssm_input.shape
    heads = step_size.shape[1]
    rows = cache_keys.shape[0]
    channels = new_keys.shape[1]
    q_heads = queries.shape[1] // ATT_DIM
    kv_here = max(1, q_heads // (ATT_HEADS // KV_HEADS))
    kvw = kv_here * ATT_DIM
    per_group = min(SSM_HEADS // GROUPS, heads)
    groups_here = heads // per_group
    limit = pltpu.CompilerParams(vmem_limit_bytes=60 * 1024 * 1024)
    shape = jax.ShapeDtypeStruct
    state, run, fade, at, gram, meta, kvc, kvn = pl.pallas_call(
        local_kernel,
        out_shape=(
            shape((STATE, width), BF16),
            shape((tokens + 16, 3 * heads), BF16),
            shape((tokens, heads), BF16),
            shape((heads, tokens), F32),
            shape((groups_here, tokens, tokens), F32),
            shape((1, width + channels), F32),
            shape((rows, 2 * kvw), BF16),
            shape((tokens, 2 * kvw), BF16),
        ),
        in_specs=[VMEM] * 13,
        out_specs=(VMEM,) * 8,
        compiler_params=limit,
        name="local",
    )(
        ssm_input,
        state_in,
        state_out,
        step_size.T,
        decay_rate.reshape(1, heads),
        forget.reshape(1, tokens),
        skip_gain.reshape(1, heads),
        new_keys,
        new_values,
        cache_keys,
        cache_values,
        cache_key_scale.reshape(1, channels),
        cache_value_scale.reshape(1, channels),
    )
    half = width // 2
    size = min(256, half)
    chunks = half // size
    n2 = n // 2
    levels = n2.bit_length() - 1
    fan = max(1, n2 // 2)
    dma = pltpu.SemaphoreType.DMA
    carried, allm, part, attended = pl.pallas_call(
        functools.partial(comm_kernel, n, chunks),
        out_shape=(
            shape((STATE, width), BF16),
            shape((n, 1, width + channels), F32),
            shape((tokens, width), BF16),
            shape((tokens, queries.shape[1]), BF16),
        ),
        in_specs=[VMEM] * 9,
        out_specs=(VMEM,) * 4,
        scratch_shapes=[
            pltpu.VMEM((n, rows, 2 * kvw), BF16),
            pltpu.VMEM((n, tokens, 2 * kvw), BF16),
            pltpu.VMEM((kv_here, n * rows, 2 * ATT_DIM), BF16),
            pltpu.VMEM((kv_here, n * tokens, 2 * ATT_DIM), BF16),
            pltpu.VMEM((tokens, n * tokens), F32),
            pltpu.VMEM((chunks, STATE, size), BF16),
            pltpu.VMEM((chunks, STATE, size), F32),
            pltpu.VMEM((levels, chunks, STATE, size), BF16),
            pltpu.VMEM((levels, chunks, STATE, size), BF16),
            pltpu.VMEM((chunks, STATE, size), BF16),
            dma((n,)),
            dma((n,)),
            dma((2, n2)),
            dma((2, n)),
            dma((2, n2)),
            dma((chunks,)),
            dma((chunks,)),
            dma((levels, chunks, fan)),
            dma((levels, chunks)),
            dma((levels, chunks)),
            dma((chunks,)),
            dma((chunks,)),
        ],
        compiler_params=pltpu.CompilerParams(
            collective_id=0, has_side_effects=True, vmem_limit_bytes=60 * 1024 * 1024
        ),
        name="exchange",
    )(state, kvc, kvn, meta, ssm_input, run, at, gram, queries)
    y, codes, scale = pl.pallas_call(
        final_kernel,
        out_shape=(
            shape((tokens, width), BF16),
            shape((tokens, channels), BF16),
            shape((1, channels), F32),
        ),
        in_specs=[VMEM] * 6,
        out_specs=(VMEM,) * 3,
        compiler_params=limit,
        name="finish",
    )(part, fade, state_out, carried, allm, new_keys)
    return (y, attended, codes, scale.reshape(channels))


def solution(mesh):
    in_specs = (
        P("seq", "head"),
        P("seq", None),
        P("seq", None),
        P("seq", "head"),
        P("head"),
        P("seq"),
        P("head"),
        P("seq", "head"),
        P("seq", None),
        P("seq", None),
        P("seq", None),
        P("seq", None),
        P(),
        P(),
    )
    out_specs = (P("seq", "head"), P("seq", "head"), P("seq", None), P())
    return jax.shard_map(
        functools.partial(body, mesh.shape["seq"]),
        mesh=mesh,
        in_specs=in_specs,
        out_specs=out_specs,
        check_vma=False,
    )
```

```python
import functools
import jax
import jax.numpy as jnp
from jax import lax
from jax.experimental import pallas as pl
from jax.experimental.pallas import tpu as pltpu
from jax.sharding import PartitionSpec as P

SSM_HEADS = 256
HEAD_DIM = 64
STATE = 256
GROUPS = 8
ATT_HEADS = 64
KV_HEADS = 8
ATT_DIM = 128

NEG = -1e30
LOG2E = 1.4426950408889634
HIGHEST = lax.Precision.HIGHEST
MESH = pl.DeviceIdType.MESH
VMEM = pl.BlockSpec(memory_space=pltpu.VMEM)
F32 = jnp.float32
BF16 = jnp.bfloat16


def iota(shape, axis):
    return lax.broadcasted_iota(jnp.int32, shape, axis)


def lanes(start, size):
    return pl.ds(pl.multiple_of(start, 128), size)


def local_kernel(
    x_ref,
    sin_ref,
    sout_ref,
    step_ref,
    decay_ref,
    forget_ref,
    skip_ref,
    nk_ref,
    nv_ref,
    ck_ref,
    cv_ref,
    cks_ref,
    cvs_ref,
    state_ref,
    run_ref,
    fade_ref,
    at_ref,
    gram_ref,
    meta_ref,
    kvc_ref,
    kvn_ref,
):
    tokens, width = x_ref.shape
    heads = step_ref.shape[0]
    per_group = min(SSM_HEADS // GROUPS, heads)
    groups_here = heads // per_group
    z = lax.axis_index("head")
    group0 = z * heads // (SSM_HEADS // GROUPS)
    kvw = kvc_ref.shape[1] // 2
    q_heads = heads * ATT_HEADS // SSM_HEADS
    first = z * q_heads // (ATT_HEADS // KV_HEADS)
    cols = lanes(first * ATT_DIM, kvw)
    kvc_ref[:, :kvw] = (ck_ref[:, cols].astype(F32) * cks_ref[:, cols]).astype(BF16)
    kvc_ref[:, kvw:] = (cv_ref[:, cols].astype(F32) * cvs_ref[:, cols]).astype(BF16)
    kvn_ref[:, :kvw] = nk_ref[:, cols]
    kvn_ref[:, kvw:] = nv_ref[:, cols]
    meta_ref[:, width:] = jnp.max(jnp.abs(nk_ref[...].astype(F32)), axis=0, keepdims=True)

    row, col = iota((tokens, tokens), 0), iota((tokens, tokens), 1)
    lower = jnp.where(col <= row, 1.0, 0.0)
    eye = jnp.where(col == row, 1.0, 0.0)
    step = step_ref[...].T
    forgotten = jnp.sum(lower * forget_ref[...], axis=1, keepdims=True)
    decayed = jnp.dot(
        lower, decay_ref[...] * step, precision=HIGHEST, preferred_element_type=F32
    )
    running = -(decayed + forgotten) * LOG2E
    start = running - jnp.log2(step)
    at_ref[...] = start.T
    rest = jnp.concatenate(
        [running, jnp.broadcast_to(skip_ref[...], (16, heads))], axis=0
    )
    for third in range(3):
        piece = rest.astype(BF16)
        run_ref[:, third * heads : (third + 1) * heads] = piece
        rest = rest - piece.astype(F32)
    fade_ref[...] = jnp.exp2(running).astype(BF16)
    tail = jnp.exp2(running[tokens - 1 : tokens] - start).astype(BF16)
    last = running[tokens - 8 : tokens]
    block = min(512, width)
    for g in range(groups_here):
        gcols = lanes((group0 + g) * STATE, STATE)
        maps_in = sin_ref[:, gcols]
        gram_ref[g] = lax.dot_general(
            sout_ref[:, gcols], maps_in, (((1,), (1,)), ((), ())), preferred_element_type=F32
        )
        turned = lax.dot_general(
            maps_in,
            eye.astype(BF16),
            (((0,), (0,)), ((), ())),
            preferred_element_type=F32,
        ).astype(BF16)
        for b in range(per_group * HEAD_DIM // block):
            begin = g * per_group * HEAD_DIM + b * block
            here = pl.ds(begin, block)
            pick = choose(heads, begin, block)
            meta_ref[:, here] = jnp.dot(
                last, pick, precision=HIGHEST, preferred_element_type=F32
            )[7:8]
            scale = jnp.dot(tail, pick.astype(BF16), preferred_element_type=F32)
            scaled = (x_ref[:, here].astype(F32) * scale).astype(BF16)
            state_ref[:, here] = jnp.dot(
                turned, scaled, preferred_element_type=F32
            ).astype(BF16)


def choose(heads, begin, size):
    lane = begin + iota((heads, size), 1)
    return (iota((heads, size), 0) == lane // HEAD_DIM).astype(F32)


def within_pair(p, x_ref, run_ref, at_ref, gram_ref, part_ref):
    tokens = x_ref.shape[0]
    heads = run_ref.shape[1] // 3
    per_group = min(SSM_HEADS // GROUPS, heads)
    here = lanes(p * 128, 128)
    pick = choose(heads, p * 128, 128).astype(BF16)
    both = jnp.dot(
        run_ref[...], jnp.concatenate([pick] * 3, axis=0), preferred_element_type=F32
    )
    run, skip = both[:tokens], both[tokens : tokens + 1]
    x = x_ref[:, here]
    gram = gram_ref[(2 * p) // per_group]
    causal = iota((tokens, tokens), 1) <= iota((tokens, tokens), 0)

    def one(k):
        spread = run[:, k * HEAD_DIM : k * HEAD_DIM + 1] - at_ref[pl.ds(2 * p + k, 1), :]
        return (jnp.exp2(jnp.where(causal, spread, NEG)) * gram).astype(BF16)

    pair = jnp.dot(
        jnp.concatenate([one(0), one(1)], axis=0), x, preferred_element_type=F32
    )
    y = jnp.where(iota((tokens, 128), 1) < HEAD_DIM, pair[:tokens], pair[tokens:])
    part_ref[:, here] = (y + skip * x.astype(F32)).astype(BF16)


def attend(h, q_ref, allc_ref, alln_ref, bias_ref, vc_ref, vn_ref, att_ref):
    q_heads = q_ref.shape[1] // ATT_DIM
    kv_here = vc_ref.shape[0]
    share = q_heads // kv_here
    together = 2 if share % 2 == 0 else 1
    tokens = q_ref.shape[0]
    k = (h * together) // share
    factor = ATT_DIM**-0.5 * LOG2E
    nt = (((1,), (1,)), ((), ()))
    own = [lanes((h * together + e) * ATT_DIM, ATT_DIM) for e in range(together)]
    q = jnp.concatenate([q_ref[:, o] for o in own], axis=0)
    at = lanes(k * ATT_DIM, ATT_DIM)
    keys_c = allc_ref[:, :, at].reshape(-1, ATT_DIM)
    keys_n = alln_ref[:, :, at].reshape(-1, ATT_DIM)
    old = lax.dot_general(q, keys_c, nt, preferred_element_type=F32)
    new = lax.dot_general(q, keys_n, nt, preferred_element_type=F32)
    bias = bias_ref[...]
    new = (new.reshape(together, tokens, -1) + bias[None]).reshape(together * tokens, -1)
    peak = jnp.maximum(
        jnp.max(old, axis=1, keepdims=True), jnp.max(new, axis=1, keepdims=True)
    )
    old = jnp.exp2((old - peak) * factor).astype(BF16)
    new = jnp.exp2((new - peak) * factor).astype(BF16)
    both = jnp.dot(old, vc_ref[k], preferred_element_type=F32) + jnp.dot(
        new, vn_ref[k], preferred_element_type=F32
    )
    result = (both[:, :ATT_DIM] / both[:, ATT_DIM:]).astype(BF16)
    for e in range(together):
        att_ref[:, own[e]] = result[e * tokens : (e + 1) * tokens]


def comm_kernel(
    n,
    chunks,
    state_ref,
    kvc_ref,
    kvn_ref,
    meta_ref,
    x_ref,
    run_ref,
    at_ref,
    gram_ref,
    q_ref,
    out_ref,
    allm_ref,
    part_ref,
    att_ref,
    allc_ref,
    alln_ref,
    vc_ref,
    vn_ref,
    bias_ref,
    sib_ref,
    own_ref,
    incl_ref,
    recv_ref,
    back_ref,
    meta_s,
    meta_r,
    kv_s,
    kv_r,
    kv_f,
    sib_s,
    sib_r,
    pre_s,
    pre_r,
    rel_s,
    back_s,
    back_r,
):
    n2 = n // 2
    levels = n2.bit_length() - 1
    me = lax.axis_index("seq")
    i, c = me % 2, me // 2
    other = me + 1 - 2 * i
    width = state_ref.shape[1]
    half = width // 2
    size = half // chunks

    barrier = pltpu.get_barrier_semaphore()
    for d in range(1, n):
        pl.semaphore_signal(
            barrier, inc=1, device_id={"seq": (me + d) % n}, device_id_type=MESH
        )
    pl.semaphore_wait(barrier, n - 1)

    def remote(src, dst, ssem, rsem, to):
        return pltpu.make_async_remote_copy(
            src_ref=src,
            dst_ref=dst,
            send_sem=ssem,
            recv_sem=rsem,
            device_id={"seq": to},
            device_id_type=MESH,
        )

    def sib_copy(j):
        return remote(
            state_ref.at[:, lanes((1 - i) * half + j * size, size)],
            sib_ref.at[j],
            sib_s.at[j],
            sib_r.at[j],
            other,
        )

    for j in range(chunks):
        sib_copy(j).start()
    for d in range(1, n):
        remote(
            meta_ref, allm_ref.at[me], meta_s.at[d], meta_r.at[me], (me + d) % n
        ).start()

    def cache_copy(d, to):
        return remote(kvc_ref, allc_ref.at[me], kv_s.at[0, d], kv_r.at[0, me], to)

    def new_copy(d, to):
        return remote(kvn_ref, alln_ref.at[me], kv_s.at[1, d], kv_r.at[1, me], to)

    cache_copy(0, other).start()
    new_copy(0, other).start()
    for d in range(1, n2):
        to = ((c + d) % n2) * 2 + i
        cache_copy(d, to).start()

        @pl.when(c + d < n2)
        def _():
            new_copy(d, to).start()

    allm_ref[me] = meta_ref[...]
    allc_ref[me] = kvc_ref[...]
    alln_ref[me] = kvn_ref[...]
    for d in range(1, n2):
        later = c + d

        @pl.when(later < n2)
        def _():
            for k in range(2):
                alln_ref[later * 2 + k] = jnp.zeros(kvn_ref.shape, BF16)

    for d in range(1, n):
        r = (me + d) % n
        remote(meta_ref, allm_ref.at[r], meta_s.at[d], meta_r.at[r], r).wait_recv()

    def sends(l):
        return c % (2 ** (l + 1)) == 2**l - 1

    def targets(l):
        return [0] if l == 0 else list(range(1, 2**l, 2))

    def pre_copy(l, j, r):
        return remote(
            incl_ref.at[l, j],
            recv_ref.at[l, j],
            pre_s.at[l, j, r],
            pre_r.at[l, j],
            ((c + 1 + r) % n2) * 2 + i,
        )

    def relay_copy(l, j):
        return remote(
            recv_ref.at[l, j],
            recv_ref.at[l, j],
            rel_s.at[l, j],
            pre_r.at[l, j],
            ((c + n2 - 1) % n2) * 2 + i,
        )

    def logs(r, j):
        return allm_ref[r, :, lanes(i * half + j * size, size)]

    def gather_first(j, _):
        sib_copy(j).wait_recv()
        mine = state_ref[:, lanes(i * half + j * size, size)].astype(F32)
        theirs = sib_ref[j].astype(F32)
        d1 = jnp.exp2(logs(2 * c + 1, j))
        total = jnp.where(i == 0, d1 * mine + theirs, d1 * theirs + mine)
        incl_ref[0, j] = total.astype(BF16)
        own_ref[j] = jnp.zeros(own_ref.shape[1:], F32)

        @pl.when(sends(0))
        def _():
            pre_copy(0, j, 0).start()

        return 0

    lax.fori_loop(0, chunks, gather_first, 0)
    fresh = bias_ref.shape[1]
    tokens = x_ref.shape[0]
    seen = iota((tokens, fresh), 1) <= me * tokens + iota((tokens, fresh), 0)
    bias_ref[...] = jnp.where(seen, 0.0, NEG)
    twin = 2 if width % 256 == 0 else 1
    pairs = width // 128 // twin
    early = n2
    ahead = pairs * 3 // 4

    def pair(p, _):
        for e in range(twin):
            within_pair(twin * p + e, x_ref, run_ref, at_ref, gram_ref, part_ref)
        return 0


    def forward(kind, d):
        src = allc_ref if kind == 0 else alln_ref
        slot = ((c + d) % n2) * 2 + i
        return remote(
            src.at[slot], src.at[slot], kv_f.at[kind, d], kv_r.at[kind, slot], other
        )

    def combine(j, _):
        for l in range(levels):

            @pl.when(c % (2 ** (l + 1)) >= 2**l)
            def _():
                pre_copy(l, j, 0).wait_recv()
                if l >= 1:

                    @pl.when(c % 2 == 1)
                    def _():
                        relay_copy(l, j).start()

                base = c - c % (2**l)
                logsum = jnp.zeros((1, size), F32)
                for back in range(1, 2**l):
                    at = (c + n2 - back) % n2
                    both = logs(2 * at, j) + logs(2 * at + 1, j)
                    logsum += jnp.where(c - back >= base, both, 0.0)
                own_ref[j] = jnp.exp2(logsum) * recv_ref[l, j].astype(F32) + own_ref[j]

            if l + 1 < levels:

                @pl.when(sends(l + 1))
                def _():
                    keep = jnp.exp2(logs(2 * c, j) + logs(2 * c + 1, j))
                    incl_ref[l + 1, j] = (
                        keep * own_ref[j] + incl_ref[0, j].astype(F32)
                    ).astype(BF16)
                    for r in targets(l + 1):
                        pre_copy(l + 1, j, r).start()

        enter = own_ref[j]
        mine = state_ref[:, lanes(i * half + j * size, size)].astype(F32)
        first = jnp.where(i == 0, mine, sib_ref[j].astype(F32))
        middle = jnp.exp2(logs(2 * c, j)) * enter + first
        out_ref[:, lanes(i * half + j * size, size)] = jnp.where(
            i == 0, enter, middle
        ).astype(BF16)
        back_ref[j] = jnp.where(i == 0, middle, enter).astype(BF16)
        back_copy(j, i).start()
        return 0

    def remote_slot(kind, d):
        src = allc_ref if kind == 0 else alln_ref
        mine = kvc_ref if kind == 0 else kvn_ref
        slot = ((c + d) % n2) * 2 + i
        return remote(mine, src.at[slot], kv_s.at[kind, d], kv_r.at[kind, slot], slot)

    def back_copy(j, who):
        return remote(
            back_ref.at[j],
            out_ref.at[:, lanes(who * half + j * size, size)],
            back_s.at[j],
            back_r.at[j],
            other,
        )

    def first_part(j, _):
        lax.fori_loop(j * ahead // early, (j + 1) * ahead // early, pair, 0)
        for d in range(1, n2):

            @pl.when(j == d)
            def _():
                remote_slot(0, d).wait_recv()
                forward(0, d).start()

                @pl.when((c + d) % n2 < c)
                def _():
                    remote_slot(1, d).wait_recv()
                    forward(1, d).start()

        return 0

    lax.fori_loop(0, early, first_part, 0)

    def other_slot(kind, d):
        src = allc_ref if kind == 0 else alln_ref
        mine = kvc_ref if kind == 0 else kvn_ref
        slot = ((c + d) % n2) * 2 + (1 - i)
        return remote(mine, src.at[slot], kv_f.at[kind, d], kv_r.at[kind, slot], other)

    for d in range(n2):
        other_slot(0, d).wait_recv()
    other_slot(1, 0).wait_recv()
    for d in range(1, n2):

        @pl.when((c + d) % n2 < c)
        def _():
            other_slot(1, d).wait_recv()

    kv_here = vc_ref.shape[0]
    for k in range(kv_here):
        at = (kv_here + k) * ATT_DIM
        for all_ref, ext_ref in ((allc_ref, vc_ref), (alln_ref, vn_ref)):
            ext_ref[k, :, :ATT_DIM] = all_ref[:, :, at : at + ATT_DIM].reshape(-1, ATT_DIM)
            ext_ref[k, :, ATT_DIM:] = jnp.ones((ext_ref.shape[1], ATT_DIM), BF16)

    q_heads = q_ref.shape[1] // ATT_DIM
    steps = q_heads // 2 if (q_heads // kv_here) % 2 == 0 else q_heads

    served = steps * 3 // 4

    def head(h, _):
        attend(h, q_ref, allc_ref, alln_ref, bias_ref, vc_ref, vn_ref, att_ref)
        return 0

    def second_part(j, _):
        rest = pairs - ahead
        lax.fori_loop(
            ahead + j * rest // chunks, ahead + (j + 1) * rest // chunks, pair, 0
        )
        lax.fori_loop(j * served // chunks, (j + 1) * served // chunks, head, 0)
        combine(j, 0)
        return 0

    lax.fori_loop(0, chunks, second_part, 0)
    lax.fori_loop(served, steps, head, 0)

    def drain(j, _):
        back_copy(j, 1 - i).wait_recv()
        back_copy(j, i).wait_send()
        sib_copy(j).wait_send()
        for l in range(levels):

            @pl.when(sends(l))
            def _():
                for r in targets(l):
                    pre_copy(l, j, r).wait_send()

            if l >= 1:

                @pl.when((c % (2 ** (l + 1)) >= 2**l) & (c % 2 == 1))
                def _():
                    relay_copy(l, j).wait_send()

        return 0

    lax.fori_loop(0, chunks, drain, 0)
    for d in range(1, n):
        remote(
            meta_ref, allm_ref.at[me], meta_s.at[d], meta_r.at[me], (me + d) % n
        ).wait_send()
    cache_copy(0, other).wait_send()
    new_copy(0, other).wait_send()
    for d in range(1, n2):
        to = ((c + d) % n2) * 2 + i
        cache_copy(d, to).wait_send()
        forward(0, d).wait_send()

        @pl.when(c + d < n2)
        def _():
            new_copy(d, to).wait_send()

        @pl.when((c + d) % n2 < c)
        def _():
            forward(1, d).wait_send()


def final_kernel(
    part_ref,
    fade_ref,
    sout_ref,
    state_ref,
    meta_ref,
    nk_ref,
    y_ref,
    code_ref,
    scale_ref,
):
    tokens, width = part_ref.shape
    heads = fade_ref.shape[1]
    per_group = min(SSM_HEADS // GROUPS, heads)
    z = lax.axis_index("head")
    group0 = z * heads // (SSM_HEADS // GROUPS)
    block = min(512, width)

    magnitude = jnp.max(meta_ref[:, 0, width:], axis=0, keepdims=True)
    scale = (magnitude + 1e-6) / 127.0
    scale_ref[...] = scale
    code_ref[...] = (nk_ref[...].astype(F32) / scale).astype(BF16)
    fade = fade_ref[...]
    for b in range(width // block):
        here = pl.ds(b * block, block)
        g = group0 + (b * block) // (per_group * HEAD_DIM)
        prior = jnp.dot(
            sout_ref[:, lanes(g * STATE, STATE)], state_ref[:, here], preferred_element_type=F32
        )
        pick = choose(heads, b * block, block).astype(BF16)
        spread = jnp.dot(fade, pick, preferred_element_type=F32)
        y_ref[:, here] = (part_ref[:, here].astype(F32) + spread * prior).astype(BF16)


def body(
    n,
    ssm_input,
    state_in,
    state_out,
    step_size,
    decay_rate,
    forget,
    skip_gain,
    queries,
    new_keys,
    new_values,
    cache_keys,
    cache_values,
    cache_key_scale,
    cache_value_scale,
):
    tokens, width = ssm_input.shape
    heads = step_size.shape[1]
    rows = cache_keys.shape[0]
    channels = new_keys.shape[1]
    q_heads = queries.shape[1] // ATT_DIM
    kv_here = max(1, q_heads // (ATT_HEADS // KV_HEADS))
    kvw = kv_here * ATT_DIM
    per_group = min(SSM_HEADS // GROUPS, heads)
    groups_here = heads // per_group
    limit = pltpu.CompilerParams(vmem_limit_bytes=60 * 1024 * 1024)
    shape = jax.ShapeDtypeStruct
    state, run, fade, at, gram, meta, kvc, kvn = pl.pallas_call(
        local_kernel,
        out_shape=(
            shape((STATE, width), BF16),
            shape((tokens + 16, 3 * heads), BF16),
            shape((tokens, heads), BF16),
            shape((heads, tokens), F32),
            shape((groups_here, tokens, tokens), F32),
            shape((1, width + channels), F32),
            shape((rows, 2 * kvw), BF16),
            shape((tokens, 2 * kvw), BF16),
        ),
        in_specs=[VMEM] * 13,
        out_specs=(VMEM,) * 8,
        compiler_params=limit,
        name="local",
    )(
        ssm_input,
        state_in,
        state_out,
        step_size.T,
        decay_rate.reshape(1, heads),
        forget.reshape(1, tokens),
        skip_gain.reshape(1, heads),
        new_keys,
        new_values,
        cache_keys,
        cache_values,
        cache_key_scale.reshape(1, channels),
        cache_value_scale.reshape(1, channels),
    )
    half = width // 2
    size = min(256, half)
    chunks = half // size
    n2 = n // 2
    levels = n2.bit_length() - 1
    fan = max(1, n2 // 2)
    dma = pltpu.SemaphoreType.DMA
    carried, allm, part, attended = pl.pallas_call(
        functools.partial(comm_kernel, n, chunks),
        out_shape=(
            shape((STATE, width), BF16),
            shape((n, 1, width + channels), F32),
            shape((tokens, width), BF16),
            shape((tokens, queries.shape[1]), BF16),
        ),
        in_specs=[VMEM] * 9,
        out_specs=(VMEM,) * 4,
        scratch_shapes=[
            pltpu.VMEM((n, rows, 2 * kvw), BF16),
            pltpu.VMEM((n, tokens, 2 * kvw), BF16),
            pltpu.VMEM((kv_here, n * rows, 2 * ATT_DIM), BF16),
            pltpu.VMEM((kv_here, n * tokens, 2 * ATT_DIM), BF16),
            pltpu.VMEM((tokens, n * tokens), F32),
            pltpu.VMEM((chunks, STATE, size), BF16),
            pltpu.VMEM((chunks, STATE, size), F32),
            pltpu.VMEM((levels, chunks, STATE, size), BF16),
            pltpu.VMEM((levels, chunks, STATE, size), BF16),
            pltpu.VMEM((chunks, STATE, size), BF16),
            dma((n,)),
            dma((n,)),
            dma((2, n2)),
            dma((2, n)),
            dma((2, n2)),
            dma((chunks,)),
            dma((chunks,)),
            dma((levels, chunks, fan)),
            dma((levels, chunks)),
            dma((levels, chunks)),
            dma((chunks,)),
            dma((chunks,)),
        ],
        compiler_params=pltpu.CompilerParams(
            collective_id=0, has_side_effects=True, vmem_limit_bytes=60 * 1024 * 1024
        ),
        name="exchange",
    )(state, kvc, kvn, meta, ssm_input, run, at, gram, queries)
    y, codes, scale = pl.pallas_call(
        final_kernel,
        out_shape=(
            shape((tokens, width), BF16),
            shape((tokens, channels), BF16),
            shape((1, channels), F32),
        ),
        in_specs=[VMEM] * 6,
        out_specs=(VMEM,) * 3,
        compiler_params=limit,
        name="finish",
    )(part, fade, state_out, carried, allm, new_keys)
    return (y, attended, codes, scale.reshape(channels))


def solution(mesh):
    in_specs = (
        P("seq", "head"),
        P("seq", None),
        P("seq", None),
        P("seq", "head"),
        P("head"),
        P("seq"),
        P("head"),
        P("seq", "head"),
        P("seq", None),
        P("seq", None),
        P("seq", None),
        P("seq", None),
        P(),
        P(),
    )
    out_specs = (P("seq", "head"), P("seq", "head"), P("seq", None), P())
    return jax.shard_map(
        functools.partial(body, mesh.shape["seq"]),
        mesh=mesh,
        in_specs=in_specs,
        out_specs=out_specs,
        check_vma=False,
    )
```

```python
import functools
import jax
import jax.numpy as jnp
from jax import lax
from jax.experimental import pallas as pl
from jax.experimental.pallas import tpu as pltpu
from jax.sharding import PartitionSpec as P

SSM_HEADS = 256
HEAD_DIM = 64
STATE = 256
GROUPS = 8
ATT_HEADS = 64
KV_HEADS = 8
ATT_DIM = 128

NEG = -1e30
LOG2E = 1.4426950408889634
HIGHEST = lax.Precision.HIGHEST
MESH = pl.DeviceIdType.MESH
VMEM = pl.BlockSpec(memory_space=pltpu.VMEM)
F32 = jnp.float32
BF16 = jnp.bfloat16


def iota(shape, axis):
    return lax.broadcasted_iota(jnp.int32, shape, axis)


def lanes(start, size):
    return pl.ds(pl.multiple_of(start, 128), size)


def local_kernel(
    x_ref,
    sin_ref,
    sout_ref,
    step_ref,
    decay_ref,
    forget_ref,
    skip_ref,
    nk_ref,
    nv_ref,
    ck_ref,
    cv_ref,
    cks_ref,
    cvs_ref,
    state_ref,
    run_ref,
    fade_ref,
    at_ref,
    gram_ref,
    meta_ref,
    kvc_ref,
    kvn_ref,
):
    tokens, width = x_ref.shape
    heads = step_ref.shape[0]
    per_group = min(SSM_HEADS // GROUPS, heads)
    groups_here = heads // per_group
    z = lax.axis_index("head")
    group0 = z * heads // (SSM_HEADS // GROUPS)
    kvw = kvc_ref.shape[1] // 2
    q_heads = heads * ATT_HEADS // SSM_HEADS
    first = z * q_heads // (ATT_HEADS // KV_HEADS)
    cols = lanes(first * ATT_DIM, kvw)
    kvc_ref[:, :kvw] = (ck_ref[:, cols].astype(F32) * cks_ref[:, cols]).astype(BF16)
    kvc_ref[:, kvw:] = (cv_ref[:, cols].astype(F32) * cvs_ref[:, cols]).astype(BF16)
    kvn_ref[:, :kvw] = nk_ref[:, cols]
    kvn_ref[:, kvw:] = nv_ref[:, cols]
    meta_ref[:, width:] = jnp.max(jnp.abs(nk_ref[...].astype(F32)), axis=0, keepdims=True)

    row, col = iota((tokens, tokens), 0), iota((tokens, tokens), 1)
    lower = jnp.where(col <= row, 1.0, 0.0)
    eye = jnp.where(col == row, 1.0, 0.0)
    step = step_ref[...].T
    forgotten = jnp.sum(lower * forget_ref[...], axis=1, keepdims=True)
    decayed = jnp.dot(
        lower, decay_ref[...] * step, precision=HIGHEST, preferred_element_type=F32
    )
    running = -(decayed + forgotten) * LOG2E
    start = running - jnp.log2(step)
    at_ref[...] = start.T
    rest = jnp.concatenate(
        [running, jnp.broadcast_to(skip_ref[...], (16, heads))], axis=0
    )
    for third in range(3):
        piece = rest.astype(BF16)
        run_ref[:, third * heads : (third + 1) * heads] = piece
        rest = rest - piece.astype(F32)
    fade_ref[...] = jnp.exp2(running).astype(BF16)
    tail = jnp.exp2(running[tokens - 1 : tokens] - start).astype(BF16)
    last = running[tokens - 8 : tokens]
    block = min(512, width)
    for g in range(groups_here):
        gcols = lanes((group0 + g) * STATE, STATE)
        maps_in = sin_ref[:, gcols]
        gram_ref[g] = lax.dot_general(
            sout_ref[:, gcols], maps_in, (((1,), (1,)), ((), ())), preferred_element_type=F32
        )
        turned = lax.dot_general(
            maps_in,
            eye.astype(BF16),
            (((0,), (0,)), ((), ())),
            preferred_element_type=F32,
        ).astype(BF16)
        for b in range(per_group * HEAD_DIM // block):
            begin = g * per_group * HEAD_DIM + b * block
            here = pl.ds(begin, block)
            pick = choose(heads, begin, block)
            meta_ref[:, here] = jnp.dot(
                last, pick, precision=HIGHEST, preferred_element_type=F32
            )[7:8]
            scale = jnp.dot(tail, pick.astype(BF16), preferred_element_type=F32)
            scaled = (x_ref[:, here].astype(F32) * scale).astype(BF16)
            state_ref[:, here] = jnp.dot(
                turned, scaled, preferred_element_type=F32
            ).astype(BF16)


def choose(heads, begin, size):
    lane = begin + iota((heads, size), 1)
    return (iota((heads, size), 0) == lane // HEAD_DIM).astype(F32)


def within_pair(p, x_ref, run_ref, at_ref, gram_ref, part_ref):
    tokens = x_ref.shape[0]
    heads = run_ref.shape[1] // 3
    per_group = min(SSM_HEADS // GROUPS, heads)
    here = lanes(p * 128, 128)
    pick = choose(heads, p * 128, 128).astype(BF16)
    both = jnp.dot(
        run_ref[...], jnp.concatenate([pick] * 3, axis=0), preferred_element_type=F32
    )
    run, skip = both[:tokens], both[tokens : tokens + 1]
    x = x_ref[:, here]
    gram = gram_ref[(2 * p) // per_group]
    causal = iota((tokens, tokens), 1) <= iota((tokens, tokens), 0)

    def one(k):
        spread = run[:, k * HEAD_DIM : k * HEAD_DIM + 1] - at_ref[pl.ds(2 * p + k, 1), :]
        return (jnp.exp2(jnp.where(causal, spread, NEG)) * gram).astype(BF16)

    pair = jnp.dot(
        jnp.concatenate([one(0), one(1)], axis=0), x, preferred_element_type=F32
    )
    y = jnp.where(iota((tokens, 128), 1) < HEAD_DIM, pair[:tokens], pair[tokens:])
    part_ref[:, here] = (y + skip * x.astype(F32)).astype(BF16)


def attend(h, q_ref, allc_ref, alln_ref, bias_ref, vc_ref, vn_ref, att_ref):
    q_heads = q_ref.shape[1] // ATT_DIM
    kv_here = vc_ref.shape[0]
    share = q_heads // kv_here
    together = 2 if share % 2 == 0 else 1
    tokens = q_ref.shape[0]
    k = (h * together) // share
    factor = ATT_DIM**-0.5 * LOG2E
    nt = (((1,), (1,)), ((), ()))
    own = [lanes((h * together + e) * ATT_DIM, ATT_DIM) for e in range(together)]
    q = jnp.concatenate([q_ref[:, o] for o in own], axis=0)
    at = lanes(k * ATT_DIM, ATT_DIM)
    keys_c = allc_ref[:, :, at].reshape(-1, ATT_DIM)
    keys_n = alln_ref[:, :, at].reshape(-1, ATT_DIM)
    old = lax.dot_general(q, keys_c, nt, preferred_element_type=F32)
    new = lax.dot_general(q, keys_n, nt, preferred_element_type=F32)
    bias = bias_ref[...]
    new = (new.reshape(together, tokens, -1) + bias[None]).reshape(together * tokens, -1)
    peak = jnp.maximum(
        jnp.max(old, axis=1, keepdims=True), jnp.max(new, axis=1, keepdims=True)
    )
    old = jnp.exp2((old - peak) * factor).astype(BF16)
    new = jnp.exp2((new - peak) * factor).astype(BF16)
    both = jnp.dot(old, vc_ref[k], preferred_element_type=F32) + jnp.dot(
        new, vn_ref[k], preferred_element_type=F32
    )
    result = (both[:, :ATT_DIM] / both[:, ATT_DIM:]).astype(BF16)
    for e in range(together):
        att_ref[:, own[e]] = result[e * tokens : (e + 1) * tokens]


def comm_kernel(
    n,
    chunks,
    state_ref,
    kvc_ref,
    kvn_ref,
    meta_ref,
    x_ref,
    run_ref,
    at_ref,
    gram_ref,
    q_ref,
    out_ref,
    allm_ref,
    part_ref,
    att_ref,
    allc_ref,
    alln_ref,
    vc_ref,
    vn_ref,
    bias_ref,
    sib_ref,
    own_ref,
    incl_ref,
    recv_ref,
    back_ref,
    meta_s,
    meta_r,
    kv_s,
    kv_r,
    kv_f,
    sib_s,
    sib_r,
    pre_s,
    pre_r,
    rel_s,
    mir_s,
    back_s,
    back_r,
):
    n2 = n // 2
    levels = n2.bit_length() - 1
    me = lax.axis_index("seq")
    i, c = me % 2, me // 2
    other = me + 1 - 2 * i
    width = state_ref.shape[1]
    half = width // 2
    size = half // chunks

    barrier = pltpu.get_barrier_semaphore()
    for d in range(1, n):
        pl.semaphore_signal(
            barrier, inc=1, device_id={"seq": (me + d) % n}, device_id_type=MESH
        )
    pl.semaphore_wait(barrier, n - 1)

    def remote(src, dst, ssem, rsem, to):
        return pltpu.make_async_remote_copy(
            src_ref=src,
            dst_ref=dst,
            send_sem=ssem,
            recv_sem=rsem,
            device_id={"seq": to},
            device_id_type=MESH,
        )

    def sib_copy(j):
        return remote(
            state_ref.at[:, lanes((1 - i) * half + j * size, size)],
            sib_ref.at[j],
            sib_s.at[j],
            sib_r.at[j],
            other,
        )

    for j in range(chunks):
        sib_copy(j).start()
    for d in range(1, n):
        remote(
            meta_ref, allm_ref.at[me], meta_s.at[d], meta_r.at[me], (me + d) % n
        ).start()

    def cache_copy(d, to):
        return remote(kvc_ref, allc_ref.at[me], kv_s.at[0, d], kv_r.at[0, me], to)

    def new_copy(d, to):
        return remote(kvn_ref, alln_ref.at[me], kv_s.at[1, d], kv_r.at[1, me], to)

    cache_copy(0, other).start()
    new_copy(0, other).start()
    for d in range(1, n2):
        to = ((c + d) % n2) * 2 + i
        cache_copy(d, to).start()

        @pl.when(c + d < n2)
        def _():
            new_copy(d, to).start()

    allm_ref[me] = meta_ref[...]
    allc_ref[me] = kvc_ref[...]
    alln_ref[me] = kvn_ref[...]
    for d in range(1, n2):
        later = c + d

        @pl.when(later < n2)
        def _():
            for k in range(2):
                alln_ref[later * 2 + k] = jnp.zeros(kvn_ref.shape, BF16)

    for d in range(1, n):
        r = (me + d) % n
        remote(meta_ref, allm_ref.at[r], meta_s.at[d], meta_r.at[r], r).wait_recv()

    def sends(l):
        return c % (2 ** (l + 1)) == 2**l - 1

    def targets(l):
        return [0] if l == 0 else list(range(1, 2**l, 2))

    def pre_copy(l, j, r):
        return remote(
            incl_ref.at[l, j],
            recv_ref.at[l, j],
            pre_s.at[l, j, r],
            pre_r.at[l, j],
            ((c + 1 + r) % n2) * 2 + i,
        )

    def relay_copy(l, j):
        return remote(
            recv_ref.at[l, j],
            recv_ref.at[l, j],
            rel_s.at[l, j],
            pre_r.at[l, j],
            ((c + n2 - 1) % n2) * 2 + i,
        )

    def mirror_copy(j):
        return remote(
            incl_ref.at[0, j],
            recv_ref.at[0, j],
            mir_s.at[j],
            pre_r.at[0, j],
            ((c + n2 - 1) % n2) * 2 + i,
        )

    def cross_copy(j):
        return remote(
            incl_ref.at[1, j],
            recv_ref.at[1, j],
            mir_s.at[j],
            pre_r.at[1, j],
            ((c + 2) % n2) * 2 + i,
        )

    def logs(r, j):
        return allm_ref[r, :, lanes(i * half + j * size, size)]

    def gather_first(j, _):
        sib_copy(j).wait_recv()
        mine = state_ref[:, lanes(i * half + j * size, size)].astype(F32)
        theirs = sib_ref[j].astype(F32)
        d1 = jnp.exp2(logs(2 * c + 1, j))
        total = jnp.where(i == 0, d1 * mine + theirs, d1 * theirs + mine)
        incl_ref[0, j] = total.astype(BF16)
        own_ref[j] = jnp.zeros(own_ref.shape[1:], F32)

        @pl.when(sends(0))
        def _():
            pre_copy(0, j, 0).start()

        if levels >= 2:

            @pl.when(c % 4 == 1)
            def _():
                mirror_copy(j).start()

        return 0

    lax.fori_loop(0, chunks, gather_first, 0)
    fresh = bias_ref.shape[1]
    tokens = x_ref.shape[0]
    seen = iota((tokens, fresh), 1) <= me * tokens + iota((tokens, fresh), 0)
    bias_ref[...] = jnp.where(seen, 0.0, NEG)
    twin = 2 if width % 256 == 0 else 1
    pairs = width // 128 // twin
    early = n2
    ahead = pairs * 3 // 4

    def pair(p, _):
        for e in range(twin):
            within_pair(twin * p + e, x_ref, run_ref, at_ref, gram_ref, part_ref)
        return 0


    def forward(kind, d):
        src = allc_ref if kind == 0 else alln_ref
        slot = ((c + d) % n2) * 2 + i
        return remote(
            src.at[slot], src.at[slot], kv_f.at[kind, d], kv_r.at[kind, slot], other
        )

    def combine(j, _):
        if levels >= 2:

            @pl.when(c % 4 == 0)
            def _():
                mirror_copy(j).wait_recv()
                nxt = (c + 1) % n2
                keep = jnp.exp2(logs(2 * nxt, j) + logs(2 * nxt + 1, j))
                incl_ref[1, j] = (
                    keep * incl_ref[0, j].astype(F32) + recv_ref[0, j].astype(F32)
                ).astype(BF16)
                cross_copy(j).start()

        for l in range(levels):

            @pl.when(c % (2 ** (l + 1)) >= 2**l)
            def _():
                pre_copy(l, j, 0).wait_recv()
                if l >= 2:

                    @pl.when(c % 2 == 1)
                    def _():
                        relay_copy(l, j).start()

                base = c - c % (2**l)
                logsum = jnp.zeros((1, size), F32)
                for back in range(1, 2**l):
                    at = (c + n2 - back) % n2
                    both = logs(2 * at, j) + logs(2 * at + 1, j)
                    logsum += jnp.where(c - back >= base, both, 0.0)
                own_ref[j] = jnp.exp2(logsum) * recv_ref[l, j].astype(F32) + own_ref[j]

            if l + 1 < levels:

                @pl.when(sends(l + 1))
                def _():
                    keep = jnp.exp2(logs(2 * c, j) + logs(2 * c + 1, j))
                    incl_ref[l + 1, j] = (
                        keep * own_ref[j] + incl_ref[0, j].astype(F32)
                    ).astype(BF16)
                    for r in targets(l + 1):
                        pre_copy(l + 1, j, r).start()

        enter = own_ref[j]
        mine = state_ref[:, lanes(i * half + j * size, size)].astype(F32)
        first = jnp.where(i == 0, mine, sib_ref[j].astype(F32))
        middle = jnp.exp2(logs(2 * c, j)) * enter + first
        out_ref[:, lanes(i * half + j * size, size)] = jnp.where(
            i == 0, enter, middle
        ).astype(BF16)
        back_ref[j] = jnp.where(i == 0, middle, enter).astype(BF16)
        back_copy(j, i).start()
        return 0

    def remote_slot(kind, d):
        src = allc_ref if kind == 0 else alln_ref
        mine = kvc_ref if kind == 0 else kvn_ref
        slot = ((c + d) % n2) * 2 + i
        return remote(mine, src.at[slot], kv_s.at[kind, d], kv_r.at[kind, slot], slot)

    def back_copy(j, who):
        return remote(
            back_ref.at[j],
            out_ref.at[:, lanes(who * half + j * size, size)],
            back_s.at[j],
            back_r.at[j],
            other,
        )

    def first_part(j, _):
        lax.fori_loop(j * ahead // early, (j + 1) * ahead // early, pair, 0)
        for d in range(1, n2):

            @pl.when(j == d)
            def _():
                remote_slot(0, d).wait_recv()
                forward(0, d).start()

                @pl.when((c + d) % n2 < c)
                def _():
                    remote_slot(1, d).wait_recv()
                    forward(1, d).start()

        return 0

    lax.fori_loop(0, early, first_part, 0)

    def other_slot(kind, d):
        src = allc_ref if kind == 0 else alln_ref
        mine = kvc_ref if kind == 0 else kvn_ref
        slot = ((c + d) % n2) * 2 + (1 - i)
        return remote(mine, src.at[slot], kv_f.at[kind, d], kv_r.at[kind, slot], other)

    for d in range(n2):
        other_slot(0, d).wait_recv()
    other_slot(1, 0).wait_recv()
    for d in range(1, n2):

        @pl.when((c + d) % n2 < c)
        def _():
            other_slot(1, d).wait_recv()

    kv_here = vc_ref.shape[0]
    for k in range(kv_here):
        at = (kv_here + k) * ATT_DIM
        for all_ref, ext_ref in ((allc_ref, vc_ref), (alln_ref, vn_ref)):
            ext_ref[k, :, :ATT_DIM] = all_ref[:, :, at : at + ATT_DIM].reshape(-1, ATT_DIM)
            ext_ref[k, :, ATT_DIM:] = jnp.ones((ext_ref.shape[1], ATT_DIM), BF16)

    q_heads = q_ref.shape[1] // ATT_DIM
    steps = q_heads // 2 if (q_heads // kv_here) % 2 == 0 else q_heads

    served = steps * 7 // 8

    def head(h, _):
        attend(h, q_ref, allc_ref, alln_ref, bias_ref, vc_ref, vn_ref, att_ref)
        return 0

    def second_part(j, _):
        rest = pairs - ahead
        lax.fori_loop(
            ahead + j * rest // chunks, ahead + (j + 1) * rest // chunks, pair, 0
        )
        lax.fori_loop(j * served // chunks, (j + 1) * served // chunks, head, 0)
        combine(j, 0)
        return 0

    lax.fori_loop(0, chunks, second_part, 0)
    lax.fori_loop(served, steps, head, 0)

    def drain(j, _):
        back_copy(j, 1 - i).wait_recv()
        back_copy(j, i).wait_send()
        sib_copy(j).wait_send()
        for l in range(levels):

            @pl.when(sends(l))
            def _():
                for r in targets(l):
                    pre_copy(l, j, r).wait_send()

            if l >= 2:

                @pl.when((c % (2 ** (l + 1)) >= 2**l) & (c % 2 == 1))
                def _():
                    relay_copy(l, j).wait_send()

        if levels >= 2:

            @pl.when(c % 4 == 1)
            def _():
                mirror_copy(j).wait_send()

            @pl.when(c % 4 == 0)
            def _():
                cross_copy(j).wait_send()

        return 0

    lax.fori_loop(0, chunks, drain, 0)
    for d in range(1, n):
        remote(
            meta_ref, allm_ref.at[me], meta_s.at[d], meta_r.at[me], (me + d) % n
        ).wait_send()
    cache_copy(0, other).wait_send()
    new_copy(0, other).wait_send()
    for d in range(1, n2):
        to = ((c + d) % n2) * 2 + i
        cache_copy(d, to).wait_send()
        forward(0, d).wait_send()

        @pl.when(c + d < n2)
        def _():
            new_copy(d, to).wait_send()

        @pl.when((c + d) % n2 < c)
        def _():
            forward(1, d).wait_send()


def final_kernel(
    part_ref,
    fade_ref,
    sout_ref,
    state_ref,
    meta_ref,
    nk_ref,
    y_ref,
    code_ref,
    scale_ref,
):
    tokens, width = part_ref.shape
    heads = fade_ref.shape[1]
    per_group = min(SSM_HEADS // GROUPS, heads)
    z = lax.axis_index("head")
    group0 = z * heads // (SSM_HEADS // GROUPS)
    block = min(512, width)

    magnitude = jnp.max(meta_ref[:, 0, width:], axis=0, keepdims=True)
    scale = (magnitude + 1e-6) / 127.0
    scale_ref[...] = scale
    code_ref[...] = (nk_ref[...].astype(F32) / scale).astype(BF16)
    fade = fade_ref[...]
    for b in range(width // block):
        here = pl.ds(b * block, block)
        g = group0 + (b * block) // (per_group * HEAD_DIM)
        prior = jnp.dot(
            sout_ref[:, lanes(g * STATE, STATE)], state_ref[:, here], preferred_element_type=F32
        )
        pick = choose(heads, b * block, block).astype(BF16)
        spread = jnp.dot(fade, pick, preferred_element_type=F32)
        y_ref[:, here] = (part_ref[:, here].astype(F32) + spread * prior).astype(BF16)


def body(
    n,
    ssm_input,
    state_in,
    state_out,
    step_size,
    decay_rate,
    forget,
    skip_gain,
    queries,
    new_keys,
    new_values,
    cache_keys,
    cache_values,
    cache_key_scale,
    cache_value_scale,
):
    tokens, width = ssm_input.shape
    heads = step_size.shape[1]
    rows = cache_keys.shape[0]
    channels = new_keys.shape[1]
    q_heads = queries.shape[1] // ATT_DIM
    kv_here = max(1, q_heads // (ATT_HEADS // KV_HEADS))
    kvw = kv_here * ATT_DIM
    per_group = min(SSM_HEADS // GROUPS, heads)
    groups_here = heads // per_group
    limit = pltpu.CompilerParams(vmem_limit_bytes=60 * 1024 * 1024)
    shape = jax.ShapeDtypeStruct
    state, run, fade, at, gram, meta, kvc, kvn = pl.pallas_call(
        local_kernel,
        out_shape=(
            shape((STATE, width), BF16),
            shape((tokens + 16, 3 * heads), BF16),
            shape((tokens, heads), BF16),
            shape((heads, tokens), F32),
            shape((groups_here, tokens, tokens), F32),
            shape((1, width + channels), F32),
            shape((rows, 2 * kvw), BF16),
            shape((tokens, 2 * kvw), BF16),
        ),
        in_specs=[VMEM] * 13,
        out_specs=(VMEM,) * 8,
        compiler_params=limit,
        name="local",
    )(
        ssm_input,
        state_in,
        state_out,
        step_size.T,
        decay_rate.reshape(1, heads),
        forget.reshape(1, tokens),
        skip_gain.reshape(1, heads),
        new_keys,
        new_values,
        cache_keys,
        cache_values,
        cache_key_scale.reshape(1, channels),
        cache_value_scale.reshape(1, channels),
    )
    half = width // 2
    size = min(256, half)
    chunks = half // size
    n2 = n // 2
    levels = n2.bit_length() - 1
    fan = max(1, n2 // 2)
    dma = pltpu.SemaphoreType.DMA
    carried, allm, part, attended = pl.pallas_call(
        functools.partial(comm_kernel, n, chunks),
        out_shape=(
            shape((STATE, width), BF16),
            shape((n, 1, width + channels), F32),
            shape((tokens, width), BF16),
            shape((tokens, queries.shape[1]), BF16),
        ),
        in_specs=[VMEM] * 9,
        out_specs=(VMEM,) * 4,
        scratch_shapes=[
            pltpu.VMEM((n, rows, 2 * kvw), BF16),
            pltpu.VMEM((n, tokens, 2 * kvw), BF16),
            pltpu.VMEM((kv_here, n * rows, 2 * ATT_DIM), BF16),
            pltpu.VMEM((kv_here, n * tokens, 2 * ATT_DIM), BF16),
            pltpu.VMEM((tokens, n * tokens), F32),
            pltpu.VMEM((chunks, STATE, size), BF16),
            pltpu.VMEM((chunks, STATE, size), F32),
            pltpu.VMEM((levels, chunks, STATE, size), BF16),
            pltpu.VMEM((levels, chunks, STATE, size), BF16),
            pltpu.VMEM((chunks, STATE, size), BF16),
            dma((n,)),
            dma((n,)),
            dma((2, n2)),
            dma((2, n)),
            dma((2, n2)),
            dma((chunks,)),
            dma((chunks,)),
            dma((levels, chunks, fan)),
            dma((levels, chunks)),
            dma((levels, chunks)),
            dma((chunks,)),
            dma((chunks,)),
            dma((chunks,)),
        ],
        compiler_params=pltpu.CompilerParams(
            collective_id=0, has_side_effects=True, vmem_limit_bytes=60 * 1024 * 1024
        ),
        name="exchange",
    )(state, kvc, kvn, meta, ssm_input, run, at, gram, queries)
    y, codes, scale = pl.pallas_call(
        final_kernel,
        out_shape=(
            shape((tokens, width), BF16),
            shape((tokens, channels), BF16),
            shape((1, channels), F32),
        ),
        in_specs=[VMEM] * 6,
        out_specs=(VMEM,) * 3,
        compiler_params=limit,
        name="finish",
    )(part, fade, state_out, carried, allm, new_keys)
    return (y, attended, codes, scale.reshape(channels))


def solution(mesh):
    in_specs = (
        P("seq", "head"),
        P("seq", None),
        P("seq", None),
        P("seq", "head"),
        P("head"),
        P("seq"),
        P("head"),
        P("seq", "head"),
        P("seq", None),
        P("seq", None),
        P("seq", None),
        P("seq", None),
        P(),
        P(),
    )
    out_specs = (P("seq", "head"), P("seq", "head"), P("seq", None), P())
    return jax.shard_map(
        functools.partial(body, mesh.shape["seq"]),
        mesh=mesh,
        in_specs=in_specs,
        out_specs=out_specs,
        check_vma=False,
    )
```
